512 devices in a mesh: head: 8 (over x, core), pos: 64 (over z, y).
Axes of the slice: x: 4, y: 8, z: 8, core: 2. Of those that a mesh axis runs over, the one named last changes fastest.
Arguments:
- ref_queries: bfloat16 [8, 512, 128], P('head', 'pos'), may hold values from -128 to 128
- query_pos: int32 [8, 512], P('head', 'pos'), may hold values from 0 to 32767, as said below
- cache_keys: bfloat16 [8, 32768, 128], P('head', 'pos'), may hold values from -8 to 8
- cache_values: bfloat16 [8, 32768, 128], P('head', 'pos'), may hold values from -24 to 24
- slot_index: int32 [8, 512], P('head'), may hold values from 0 to 32767, as said below
Outputs:
- ref_output: bfloat16 [8, 512, 128], P('head', 'pos')
- compact_values: float32 [8, 512, 128], P('head')
The draws below stay inside these ranges and needn't reach their ends.
Inputs may be any that keep to these rules, and one draw needn't show every extreme that they name: `query_pos`: along each head's rows the positions never fall; the first is 0 and the last 32767. `slot_index`: within a head the slots hold distinct positions; slot 0 holds position 0 and slot 1 holds position 32767.
All inputs are finite; a program needn't handle non-finite values.
Results may differ from the reference program's by a relative error of at most 0.0042.
Values may be sent and summed in bfloat16 or wider, within the bound.
A program may use at most 64 MiB of HBM per device.

```python
import math
import jax
import jax.numpy as jnp
from jax import lax

DH = 128
KVH = 8
SLOTS = 512
POS_DEV = 512
S = 32768
NQ = 512
N_POS = 64


def slot_table(key):

    def head_slots(head_key):
        shuffled = jax.random.permutation(head_key, S - 2)[:SLOTS - 2] + 1
        return jnp.concatenate([jnp.zeros((1,), jnp.int32), jnp.full((1,), S - 1, jnp.int32), shuffled.astype(jnp.int32)])
    head_keys = jax.random.split(jax.random.fold_in(key, 5), KVH)
    return jax.vmap(head_slots)(head_keys)


def draw_slot_index(key, part):
    return slot_table(key)


def draw_query_pos(key, part):
    raw_pos = jax.random.randint(jax.random.fold_in(key, 41), (KVH, NQ), 0, S)
    ordered = jnp.sort(raw_pos, axis=1)
    ordered = ordered.at[:, 0].set(0).at[:, NQ - 1].set(S - 1)
    return ordered.astype(jnp.int32)


def draw_cache_keys(key, part):
    base = jnp.clip(jax.random.normal(jax.random.fold_in(key, 21), (KVH, S, DH), jnp.float32), -5.0, 5.0)
    return base.astype(jnp.bfloat16)


def draw_ref_queries(key, part):
    noise = jnp.clip(jax.random.normal(jax.random.fold_in(key, 31), (KVH, NQ, DH), jnp.float32), -5.0, 5.0) * 3.0
    return noise.astype(jnp.bfloat16)


def shard_levels(stream_key, dims, shards, low, high):
    factor_of, own = 1.0, jax.random.fold_in(stream_key, 6)
    for position, blocks in shards:
        draws = jnp.exp(jax.random.uniform(jax.random.fold_in(own, position), (blocks,), jnp.float32, low / len(shards), high / len(shards)))
        factor_of = factor_of * jnp.repeat(draws, dims[position] // blocks).reshape([-1 if axis == position else 1 for axis in range(len(dims))])
    return factor_of


def scatter_about(rng, shape, spread, bound, cuts=(), kind=jnp.bfloat16):
    loudness = shard_levels(rng, shape, cuts, -0.22, 0.18) if cuts else 1.0
    values = jax.random.normal(rng, shape, jnp.float32) * spread * loudness
    return jnp.minimum(jnp.maximum(values, -bound), bound).astype(kind)


def setup_inputs(seed: int = 0) -> dict:
    seeds = jax.random.split(jax.random.key(seed), 6)
    return {
        "ref_queries": draw_ref_queries(jax.random.fold_in(seeds[5], 71), 0),
        "query_pos": draw_query_pos(jax.random.fold_in(seeds[5], 71), 0),
        "cache_keys": draw_cache_keys(jax.random.fold_in(seeds[5], 71), 0),
        "cache_values": scatter_about(seeds[3], (KVH, S, DH), 4.0, 24.0, ((0, 8), (1, 64))),
        "slot_index": draw_slot_index(jax.random.fold_in(seeds[5], 71), 0),
    }


RIDGE = 1.0
NEG_FILL = -1e+30

def block_partials(query_block, qpos_block, key_block, value_block, key_base, inv_root):
    scores = jnp.dot(query_block.astype(jnp.float32), key_block.T.astype(jnp.float32), preferred_element_type=jnp.float32) * inv_root
    key_pos = key_base + jnp.arange(key_block.shape[0], dtype=jnp.int32)
    allowed = key_pos[None, :] <= qpos_block[:, None]
    masked = jnp.where(allowed, scores, NEG_FILL)
    block_top = lax.optimization_barrier(jnp.max(masked, axis=1))
    weights = jnp.where(allowed, jnp.exp(masked - block_top[:, None]), 0.0)
    weight_sum = lax.optimization_barrier(jnp.sum(weights, axis=1))
    numerators = jnp.dot(weights.astype(jnp.bfloat16).astype(jnp.float32), value_block.astype(jnp.float32), preferred_element_type=jnp.float32)
    return (block_top, weight_sum, numerators)

def feature_terms(query_rows, qpos_rows, out_rows, compact, slot_pos, inv_root):
    logits = jnp.dot(query_rows.astype(jnp.float32), compact.T.astype(jnp.float32), preferred_element_type=jnp.float32) * inv_root
    allowed = slot_pos[None, :] <= qpos_rows[:, None]
    masked = jnp.where(allowed, logits, NEG_FILL)
    row_top = lax.optimization_barrier(jnp.max(masked, axis=1, keepdims=True))
    raw_weights = jnp.where(allowed, jnp.exp(masked - row_top), 0.0)
    features = (raw_weights / lax.optimization_barrier(jnp.sum(raw_weights, axis=1, keepdims=True))).astype(jnp.bfloat16)
    gram_sum = jnp.dot(features.T.astype(jnp.float32), features.astype(jnp.float32), preferred_element_type=jnp.float32)
    cross_sum = jnp.dot(features.T.astype(jnp.float32), out_rows.astype(jnp.float32), preferred_element_type=jnp.float32)
    return (gram_sum, cross_sum)

def ridge_solve(gram_sum, cross_sum):
    identity = jnp.eye(gram_sum.shape[0], dtype=jnp.float32)
    factor_low = jnp.linalg.cholesky(gram_sum + RIDGE * identity)
    return jax.scipy.linalg.cho_solve((factor_low, True), cross_sum)

def one_head(head_data):
    queries, qpos, head_keys, head_values, slots = head_data
    inv_root = 1.0 / math.sqrt(DH)

    def visit_block(running, block_id):
        run_top, run_sum, run_numer = running
        key_base = (block_id * POS_DEV).astype(jnp.int32)
        key_block = lax.dynamic_slice_in_dim(head_keys, key_base, POS_DEV, 0)
        value_block = lax.dynamic_slice_in_dim(head_values, key_base, POS_DEV, 0)
        block_top, weight_sum, numerators = block_partials(queries, qpos, key_block, value_block, key_base, inv_root)
        new_top = jnp.maximum(run_top, block_top)
        scale_old = jnp.exp(run_top - new_top)
        scale_new = jnp.exp(block_top - new_top)
        run_sum = run_sum * scale_old + weight_sum * scale_new
        run_numer = run_numer * scale_old[:, None] + numerators * scale_new[:, None]
        return ((new_top, run_sum, run_numer), None)
    start = (jnp.full((NQ,), NEG_FILL, jnp.float32), jnp.zeros((NQ,), jnp.float32), jnp.zeros((NQ, DH), jnp.float32))
    (run_top, run_sum, run_numer), _ = lax.scan(visit_block, start, jnp.arange(N_POS, dtype=jnp.int32))
    attended = (run_numer / run_sum[:, None]).astype(jnp.bfloat16)
    compact = head_keys[slots.astype(jnp.int32)]
    gram_sum, cross_sum = feature_terms(queries, qpos, attended, compact, slots, inv_root)
    return (attended, ridge_solve(gram_sum, cross_sum))

def reference(ref_queries, query_pos, cache_keys, cache_values, slot_index):
    ref_output, compact_values = lax.map(one_head, (ref_queries, query_pos, cache_keys, cache_values, slot_index))
    return (ref_output, compact_values)
```

```python
import math

import jax
import jax.numpy as jnp
from jax import lax
from jax.experimental import pallas as pl
from jax.experimental.pallas import tpu as pltpu
from jax.sharding import PartitionSpec as P

RIDGE = 1.0
NEG_FILL = -1e30
RING = 8
BLOCK = 512
DH = 128
LANES = 128
CHUNKS = BLOCK // LANES
SLAB = DH // RING
INV_ROOT = 1.0 / math.sqrt(DH)
MESH_ID = pl.DeviceIdType.MESH
F32 = jnp.float32
BF16 = jnp.bfloat16


def dot(a, b, ca, cb, precision=None):
    return lax.dot_general(a, b, (((ca,), (cb,)), ((), ())), precision=precision, preferred_element_type=F32)


def chunk(c):
    return slice(c * LANES, (c + 1) * LANES)


def exchange_kernel(
    qpos_ref, q_ref, k_ref, v_ref, slots_ref,
    q_out, qp_out, ct_out, ot_out, own_out,
    q_y, q_z, qp_y, qp_z, c_local, c_z, c_y, c_g, vt, n_send, n_z, s_z, n_y, s_y, o_g,
    send_sems, recv_sems,
):
    me = lax.axis_index("pos")
    y = lax.rem(me, RING)
    z = lax.div(me, RING)

    def y_peer(o):
        return {"pos": z * RING + lax.rem(y + o, RING)}

    def z_peer(o):
        return {"pos": lax.rem(z + o, RING) * RING + y}

    offsets = range(1, RING)
    barrier = pltpu.get_barrier_semaphore()
    for o in offsets:
        pl.semaphore_signal(barrier, inc=1, device_id=y_peer(o), device_id_type=MESH_ID)
        pl.semaphore_signal(barrier, inc=1, device_id=z_peer(o), device_id_type=MESH_ID)

    base = me * BLOCK
    position = lax.broadcasted_iota(jnp.int32, (BLOCK, BLOCK), 0) + base
    one_hot = jnp.where(position == slots_ref[...], 1.0, 0.0).astype(BF16)
    c_local[...] = dot(k_ref[...], one_hot, 0, 0).astype(BF16).reshape(RING, SLAB, BLOCK)
    q_y[y] = q_ref[...].astype(F32)
    lane_id = lax.broadcasted_iota(jnp.int32, (RING, LANES), 0) * LANES + lax.broadcasted_iota(jnp.int32, (RING, LANES), 1)
    tile = jnp.zeros((RING, LANES), jnp.int32)
    for i in range(RING):
        tile = jnp.where(lane_id == me * RING + i, qpos_ref[0, i], tile)
    qp_y[0] = tile
    vt[...] = v_ref[...].astype(F32).T.astype(BF16)

    started = []

    def send(stream, o, src, dst, peer):
        copy = pltpu.make_async_remote_copy(
            src_ref=src, dst_ref=dst, send_sem=send_sems.at[stream, o], recv_sem=recv_sems.at[stream, o],
            device_id=peer, device_id_type=MESH_ID,
        )
        copy.start()
        started.append(copy)
        return copy

    def arrive(copies):
        for copy in copies:
            copy.wait_recv()

    pl.semaphore_wait(barrier, 2 * (RING - 1))

    get_q = [send(0, o, q_y.at[y], q_y.at[y], y_peer(o)) for o in offsets]
    get_qp = [send(1, o, qp_y.at[0], qp_y.at[o], y_peer(o)) for o in offsets]
    get_c = [send(2, o, c_local.at[lax.rem(z + o, RING)], c_z.at[o], z_peer(o)) for o in offsets]

    arrive(get_q)
    q_z[z] = q_y[...].reshape(RING * RING, DH).astype(BF16)
    get_q = [send(3, o, q_z.at[z], q_z.at[z], z_peer(o)) for o in offsets]
    arrive(get_qp)
    qp_z[0] = sum((qp_y[o] for o in offsets), qp_y[0])
    get_qp = [send(4, o, qp_z.at[0], qp_z.at[o], z_peer(o)) for o in offsets]

    arrive(get_c)
    c_y[0] = sum((c_z[o].astype(F32) for o in offsets), c_local[z].astype(F32)).astype(BF16)
    get_c = [send(5, o, c_y.at[0], c_y.at[o], y_peer(o)) for o in offsets]

    arrive(get_q)
    arrive(get_qp)
    qp = sum((qp_z[o] for o in offsets), qp_z[0])
    qp_out[...] = qp
    q_out[...] = q_z[...].reshape(BLOCK, DH)

    arrive(get_c)
    c_g[z] = sum((c_y[o].astype(F32) for o in offsets), c_y[0].astype(F32)).astype(BF16)
    get_c = [send(6, o, c_g.at[z], c_g.at[z], z_peer(o)) for o in offsets]

    key_pos = lax.broadcasted_iota(jnp.int32, (BLOCK, LANES), 0) + base
    tops, totals = [], []
    for c in range(CHUNKS):
        scores = dot(k_ref[...], q_out[chunk(c), :], 1, 1) * INV_ROOT
        allowed = key_pos <= qp[c:c + 1, :]
        masked = jnp.where(allowed, scores, NEG_FILL)
        top = jnp.max(masked, axis=0, keepdims=True)
        weights = jnp.where(allowed, jnp.exp(masked - top), 0.0)
        tops.append(top)
        totals.append(jnp.sum(weights, axis=0, keepdims=True))
        n_send[:, :, chunk(c)] = dot(vt[...], weights.astype(BF16), 1, 0).reshape(RING, SLAB, LANES)
    s_z[0] = jnp.concatenate(tops + totals, axis=0)

    get_s = [send(7, o, s_z.at[0], s_z.at[o], z_peer(o)) for o in offsets]
    get_n = [send(8, o, n_send.at[lax.rem(z + o, RING)], n_z.at[o], z_peer(o)) for o in offsets]

    def merge(stats, first, others):
        top_of = stats[0][:CHUNKS]
        for tile in stats[1:]:
            top_of = jnp.maximum(top_of, tile[:CHUNKS])
        scales = [jnp.exp(tile[:CHUNKS] - top_of) for tile in stats]
        total_of = sum(s * tile[CHUNKS:] for s, tile in zip(scales, stats))
        numers = []
        for c in range(CHUNKS):
            numer = first[:, chunk(c)] * scales[0][c:c + 1]
            for o in offsets:
                numer = numer + others[o, :, chunk(c)] * scales[o][c:c + 1]
            numers.append(numer)
        return top_of, total_of, numers

    arrive(get_s)
    arrive(get_n)
    top_z, total_z, numer_z = merge([s_z[o] for o in range(RING)], n_send.at[z], n_z)
    s_y[0] = jnp.concatenate([top_z, total_z], axis=0)
    for c in range(CHUNKS):
        n_y[0, :, chunk(c)] = numer_z[c]
    get_s = [send(9, o, s_y.at[0], s_y.at[o], y_peer(o)) for o in offsets]
    get_n = [send(10, o, n_y.at[0], n_y.at[o], y_peer(o)) for o in offsets]

    arrive(get_s)
    arrive(get_n)
    _, total, numer = merge([s_y[o] for o in range(RING)], n_y.at[0], n_y)
    for c in range(CHUNKS):
        o_g[z, :, chunk(c)] = (numer[c] / total[c:c + 1]).astype(BF16)
    get_o = [send(11, o, o_g.at[z], o_g.at[z], z_peer(o)) for o in offsets]

    arrive(get_c)
    ct_out[...] = c_g[...].reshape(DH, BLOCK)
    arrive(get_o)
    attended = o_g[...].reshape(DH, BLOCK)
    ot_out[...] = attended
    own_row = lax.broadcasted_iota(jnp.int32, (RING, BLOCK), 0) + me * RING
    pick = jnp.where(lax.broadcasted_iota(jnp.int32, (RING, BLOCK), 1) == own_row, 1.0, 0.0).astype(BF16)
    own_out[...] = dot(pick, attended, 1, 1).astype(BF16)
    for copy in started:
        copy.wait_send()


STREAMS = 12


def exchange(queries, qpos, keys, values, slots):
    vmem = pl.BlockSpec(memory_space=pltpu.VMEM)
    table = pltpu.VMEM((RING, SLAB, BLOCK), BF16)
    wide = pltpu.VMEM((RING, SLAB, BLOCK), F32)
    return pl.pallas_call(
        exchange_kernel,
        out_shape=(
            jax.ShapeDtypeStruct((BLOCK, DH), BF16),
            jax.ShapeDtypeStruct((RING, LANES), jnp.int32),
            jax.ShapeDtypeStruct((DH, BLOCK), BF16),
            jax.ShapeDtypeStruct((DH, BLOCK), BF16),
            jax.ShapeDtypeStruct((RING, DH), BF16),
        ),
        in_specs=[pl.BlockSpec(memory_space=pltpu.SMEM), vmem, vmem, vmem, vmem],
        out_specs=(vmem,) * 5,
        scratch_shapes=[
            pltpu.VMEM((RING, RING, DH), F32),
            pltpu.VMEM((RING, RING * RING, DH), BF16),
            pltpu.VMEM((RING, RING, LANES), jnp.int32),
            pltpu.VMEM((RING, RING, LANES), jnp.int32),
            table, table, table, table,
            pltpu.VMEM((DH, BLOCK), BF16),
            wide, wide,
            pltpu.VMEM((RING, 2 * CHUNKS, LANES), F32),
            wide,
            pltpu.VMEM((RING, 2 * CHUNKS, LANES), F32),
            table,
            pltpu.SemaphoreType.DMA((STREAMS, RING)),
            pltpu.SemaphoreType.DMA((STREAMS, RING)),
        ],
        compiler_params=pltpu.CompilerParams(collective_id=0, has_side_effects=True),
        name="exchange",
    )(qpos, queries, keys, values, slots)


def invert_spd(a):
    n = a.shape[0]
    row_id = lax.broadcasted_iota(jnp.int32, (8, n), 0)
    lane = lax.broadcasted_iota(jnp.int32, (8, n), 1)
    rows = [a[8 * g:8 * g + 8, :] for g in range(n // 8)]
    for k in range(0, n, 4):
        g0, s0 = divmod(k, 8)
        pivot = rows[g0]
        cols = [[jnp.broadcast_to(r[:, k + b:k + b + 1], (8, n)) for b in range(4)] for r in rows]

        def entry(i, j):
            return jnp.broadcast_to(cols[g0][j][s0 + i:s0 + i + 1, :], (8, n))

        p = {(i, j): entry(i, j) for i in range(4) for j in range(i + 1)}
        d0 = 1.0 / (p[0, 0] * p[1, 1] - p[1, 0] * p[1, 0])
        i00, i11, i10 = p[1, 1] * d0, p[0, 0] * d0, -p[1, 0] * d0
        t00, t01 = p[2, 0] * i00 + p[2, 1] * i10, p[2, 0] * i10 + p[2, 1] * i11
        t10, t11 = p[3, 0] * i00 + p[3, 1] * i10, p[3, 0] * i10 + p[3, 1] * i11
        s00 = p[2, 2] - (t00 * p[2, 0] + t01 * p[2, 1])
        s10 = p[3, 2] - (t10 * p[2, 0] + t11 * p[2, 1])
        s11 = p[3, 3] - (t10 * p[3, 0] + t11 * p[3, 1])
        d1 = 1.0 / (s00 * s11 - s10 * s10)
        j00, j11, j10 = s11 * d1, s00 * d1, -s10 * d1
        w = [jnp.broadcast_to(pivot[s0 + i:s0 + i + 1, :], (8, n)) for i in range(4)]
        w = [jnp.where(lane == k + i, 1.0, jnp.where((lane >= k) & (lane < k + 4), 0.0, w[i])) for i in range(4)]
        u2 = w[2] - (t00 * w[0] + t01 * w[1])
        u3 = w[3] - (t10 * w[0] + t11 * w[1])
        x2 = j00 * u2 + j10 * u3
        x3 = j10 * u2 + j11 * u3
        v0 = w[0] - (p[2, 0] * x2 + p[3, 0] * x3)
        v1 = w[1] - (p[2, 1] * x2 + p[3, 1] * x3)
        x0 = i00 * v0 + i10 * v1
        x1 = i10 * v0 + i11 * v1
        x = [x0, x1, x2, x3]
        own_cols = (lane >= k) & (lane < k + 4)
        new_rows = []
        for g, r in enumerate(rows):
            kept = jnp.where(own_cols, 0.0, r)
            new = kept - ((cols[g][0] * x[0] + cols[g][1] * x[1]) + (cols[g][2] * x[2] + cols[g][3] * x[3]))
            if g == g0:
                for i in range(4):
                    new = jnp.where(row_id == s0 + i, x[i], new)
            new_rows.append(new)
        rows = new_rows
    return jnp.concatenate(rows, axis=0)


def fit_kernel(q_ref, qp_ref, ct_ref, ot_ref, slots_ref, fitted_ref, feats, gram):
    keys = ct_ref[...].astype(F32).T.astype(BF16)
    slot_col = jnp.concatenate(
        [jnp.broadcast_to(slots_ref[:, chunk(c)], (LANES, LANES)).T for c in range(CHUNKS)], axis=0
    )
    for c in range(CHUNKS):
        logits = dot(keys, q_ref[chunk(c), :], 1, 1) * INV_ROOT
        allowed = slot_col <= qp_ref[c:c + 1, :]
        masked = jnp.where(allowed, logits, NEG_FILL)
        top = jnp.max(masked, axis=0, keepdims=True)
        raw = jnp.where(allowed, jnp.exp(masked - top), 0.0)
        feats[:, chunk(c)] = (raw / jnp.sum(raw, axis=0, keepdims=True)).astype(BF16)
    ft = feats[...]
    gram[:, :BLOCK] = dot(ft, ft, 1, 1)
    diagonal = lax.broadcasted_iota(jnp.int32, (LANES, LANES), 0) == lax.broadcasted_iota(jnp.int32, (LANES, LANES), 1)
    for c in range(CHUNKS):
        gram[chunk(c), chunk(c)] = gram[chunk(c), chunk(c)] + jnp.where(diagonal, RIDGE, 0.0)
    gram[:, BLOCK:] = ft.astype(F32)

    def eliminate(b, carry):
        rows = pl.ds(pl.multiple_of(b * LANES, LANES), LANES)
        inverse = invert_spd(gram[rows, rows])
        panel = dot(inverse, gram[rows, :], 1, 0, lax.Precision.HIGHEST)
        for c in range(CHUNKS):
            @pl.when(b == c)
            def _():
                gram[chunk(c), :] = panel

            @pl.when(b != c)
            def _():
                gram[chunk(c), :] = gram[chunk(c), :] - dot(gram[chunk(c), rows], panel, 1, 0, lax.Precision.HIGHEST)
        return carry

    lax.fori_loop(0, CHUNKS, eliminate, 0)
    solved = gram[:, BLOCK:]
    high = solved.astype(BF16)
    low = (solved - high.astype(F32)).astype(BF16)
    attended = ot_ref[...]
    fitted_ref[...] = dot(high, attended, 1, 1) + dot(low, attended, 1, 1)


def fit(queries, qp, ct, ot, slots):
    vmem = pl.BlockSpec(memory_space=pltpu.VMEM)
    return pl.pallas_call(
        fit_kernel,
        out_shape=jax.ShapeDtypeStruct((BLOCK, DH), F32),
        in_specs=[vmem] * 5,
        out_specs=vmem,
        scratch_shapes=[pltpu.VMEM((BLOCK, BLOCK), BF16), pltpu.VMEM((BLOCK, 2 * BLOCK), F32)],
        name="fit",
    )(queries, qp, ct, ot, slots)


def shards(ref_queries, query_pos, cache_keys, cache_values, slot_index):
    queries, qp, ct, ot, own = exchange(
        ref_queries[0], query_pos, cache_keys[0], cache_values[0], slot_index
    )
    fitted = fit(queries, qp, ct, ot, slot_index)
    return (own[None], fitted[None])


def solution(mesh):
    in_specs = (
        P("head", "pos", None),
        P("head", "pos"),
        P("head", "pos", None),
        P("head", "pos", None),
        P("head", None),
    )
    out_specs = (P("head", "pos", None), P("head", None, None))
    return jax.shard_map(shards, mesh=mesh, in_specs=in_specs, out_specs=out_specs, check_vma=False)
```

```python
import math

import jax
import jax.numpy as jnp
from jax import lax
from jax.experimental import pallas as pl
from jax.experimental.pallas import tpu as pltpu
from jax.sharding import PartitionSpec as P

RIDGE = 1.0
NEG_FILL = -1e30
RING = 8
BLOCK = 512
DH = 128
LANES = 128
CHUNKS = BLOCK // LANES
SLAB = DH // RING
INV_ROOT = 1.0 / math.sqrt(DH)
MESH_ID = pl.DeviceIdType.MESH
F32 = jnp.float32
BF16 = jnp.bfloat16


def dot(a, b, ca, cb, precision=None):
    return lax.dot_general(a, b, (((ca,), (cb,)), ((), ())), precision=precision, preferred_element_type=F32)


def chunk(c):
    return slice(c * LANES, (c + 1) * LANES)


def exact(a, b, ca, cb):
    return dot(a, b, ca, cb, lax.Precision.HIGHEST)


def invert_spd(a):
    n = a.shape[0]
    sub = lax.broadcasted_iota(jnp.int32, (8, n), 0)
    lane = lax.broadcasted_iota(jnp.int32, (8, n), 1)

    def along(v, j):
        return jnp.broadcast_to(v[:, j:j + 1], (8, n))

    def down(v, i):
        return jnp.broadcast_to(v[i:i + 1, :], (8, n))

    rows = [a[8 * g:8 * g + 8, :] for g in range(n // 8)]
    for g0 in range(n // 8):
        k = 8 * g0
        m = [jnp.where(lane < n + j, along(rows[g0], k + j), 0.0) for j in range(8)]
        for t in range(0, 8, 2):
            p00, p10, p11 = down(m[t], t), down(m[t], t + 1), down(m[t + 1], t + 1)
            scale = 1.0 / (p00 * p11 - p10 * p10)
            i00, i11, i10 = p11 * scale, p00 * scale, -(p10 * scale)
            new = []
            for j in range(8):
                if j == t:
                    kept, x0, x1 = None, i00, i10
                elif j == t + 1:
                    kept, x0, x1 = None, i10, i11
                else:
                    w0, w1 = down(m[j], t), down(m[j], t + 1)
                    kept, x0, x1 = m[j], i00 * w0 + i10 * w1, i10 * w0 + i11 * w1
                taken = m[t] * x0 + m[t + 1] * x1
                rest = -taken if kept is None else kept - taken
                new.append(jnp.where(sub == t, x0, jnp.where(sub == t + 1, x1, rest)))
            m = new
        own = (lane >= k) & (lane < k + 8)
        w = jnp.where(own, jnp.where(lane - k == sub, 1.0, 0.0), rows[g0])
        terms = [m[j] * down(w, j) for j in range(8)]
        while len(terms) > 1:
            terms = [u + v for u, v in zip(terms[::2], terms[1::2])]
        x = terms[0]
        xs = [down(x, j) for j in range(8)]
        updated = []
        for g, r in enumerate(rows):
            if g == g0:
                updated.append(x)
                continue
            terms = [along(r, k + j) * xs[j] for j in range(8)]
            while len(terms) > 1:
                terms = [u + v for u, v in zip(terms[::2], terms[1::2])]
            updated.append(jnp.where(own, 0.0, r) - terms[0])
        rows = updated
    return jnp.concatenate(rows, axis=0)


def compaction_kernel(
    qpos_hbm, q_hbm, k_hbm, v_hbm, slots_hbm,
    own_out, fitted_ref,
    qpos_ref, q_ref, k_ref, v_ref, slots_ref,
    q_y, q_z, qp_y, qp_z, c_local, c_z, c_y, c_g, vt, n_send, n_z, s_z, n_y, s_y, o_g,
    feats, gram, inverse, lower, upper,
    load_sems, send_sems, recv_sems,
):
    me = lax.axis_index("pos")
    y = lax.rem(me, RING)
    z = lax.div(me, RING)

    def y_peer(o):
        return {"pos": z * RING + lax.rem(y + o, RING)}

    def z_peer(o):
        return {"pos": lax.rem(z + o, RING) * RING + y}

    offsets = range(1, RING)
    barrier = pltpu.get_barrier_semaphore()
    for o in offsets:
        pl.semaphore_signal(barrier, inc=1, device_id=y_peer(o), device_id_type=MESH_ID)
        pl.semaphore_signal(barrier, inc=1, device_id=z_peer(o), device_id_type=MESH_ID)

    loads = [
        pltpu.make_async_copy(src, dst, load_sems.at[i])
        for i, (src, dst) in enumerate([
            (slots_hbm, slots_ref), (k_hbm, k_ref), (qpos_hbm, qpos_ref), (q_hbm, q_ref), (v_hbm, v_ref),
        ])
    ]
    for load in loads:
        load.start()
    for load in loads[:4]:
        load.wait()

    base = me * BLOCK
    position = lax.broadcasted_iota(jnp.int32, (BLOCK, BLOCK), 0) + base
    one_hot = jnp.where(position == slots_ref[...], 1.0, 0.0).astype(BF16)
    c_local[...] = dot(k_ref[...], one_hot, 0, 0).astype(BF16).reshape(RING, SLAB, BLOCK)
    q_y[y] = q_ref[...].astype(F32)
    lane_id = lax.broadcasted_iota(jnp.int32, (RING, LANES), 0) * LANES + lax.broadcasted_iota(jnp.int32, (RING, LANES), 1)
    tile = jnp.zeros((RING, LANES), jnp.int32)
    for i in range(RING):
        tile = jnp.where(lane_id == me * RING + i, qpos_ref[0, i], tile)
    qp_y[0] = tile
    loads[4].wait()
    vt[...] = v_ref[...].astype(F32).T.astype(BF16)

    started = []

    def copy_of(stream, o, src, dst, peer):
        return pltpu.make_async_remote_copy(
            src_ref=src, dst_ref=dst, send_sem=send_sems.at[stream, o], recv_sem=recv_sems.at[stream, o],
            device_id=peer, device_id_type=MESH_ID,
        )

    def send(stream, o, src, dst, peer):
        copy = copy_of(stream, o, src, dst, peer)
        copy.start()
        started.append(copy)
        return copy

    def arrive(copies):
        for copy in copies:
            copy.wait_recv()

    pl.semaphore_wait(barrier, 2 * (RING - 1))

    get_q = [send(0, o, q_y.at[y], q_y.at[y], y_peer(o)) for o in offsets]
    get_qp = [send(1, o, qp_y.at[0], qp_y.at[o], y_peer(o)) for o in offsets]
    get_c = [send(2, o, c_local.at[lax.rem(z + o, RING)], c_z.at[o], z_peer(o)) for o in offsets]

    arrive(get_q)
    q_z[z] = q_y[...].reshape(RING * RING, DH).astype(BF16)
    get_q = [send(3, o, q_z.at[z], q_z.at[z], z_peer(o)) for o in offsets]
    arrive(get_qp)
    qp_z[0] = sum((qp_y[o] for o in offsets), qp_y[0])
    get_qp = [send(4, o, qp_z.at[0], qp_z.at[o], z_peer(o)) for o in offsets]

    arrive(get_c)
    c_y[0] = sum((c_z[o].astype(F32) for o in offsets), c_local[z].astype(F32)).astype(BF16)
    get_c = [send(5, o, c_y.at[0], c_y.at[o], y_peer(o)) for o in offsets]

    arrive(get_q)
    arrive(get_qp)
    qp = sum((qp_z[o] for o in offsets), qp_z[0])
    queries = q_z[...].reshape(BLOCK, DH)

    arrive(get_c)
    c_g[z] = sum((c_y[o].astype(F32) for o in offsets), c_y[0].astype(F32)).astype(BF16)
    get_c = [send(6, o, c_g.at[z], c_g.at[z], z_peer(o)) for o in offsets]

    key_pos = lax.broadcasted_iota(jnp.int32, (BLOCK, LANES), 0) + base
    tops, totals = [], []
    for c in range(CHUNKS):
        scores = dot(k_ref[...], queries[chunk(c), :], 1, 1) * INV_ROOT
        allowed = key_pos <= qp[c:c + 1, :]
        masked = jnp.where(allowed, scores, NEG_FILL)
        top = jnp.max(masked, axis=0, keepdims=True)
        weights = jnp.where(allowed, jnp.exp(masked - top), 0.0)
        tops.append(top)
        totals.append(jnp.sum(weights, axis=0, keepdims=True))
        n_send[:, :, chunk(c)] = dot(vt[...], weights.astype(BF16), 1, 0).reshape(RING, SLAB, LANES)
    s_z[0] = jnp.concatenate(tops + totals, axis=0)

    get_s = [send(7, o, s_z.at[0], s_z.at[o], z_peer(o)) for o in offsets]
    get_n = [send(8, o, n_send.at[lax.rem(z + o, RING)], n_z.at[o], z_peer(o)) for o in offsets]

    def merge(stats, first, others):
        top_of = stats[0][:CHUNKS]
        for tile in stats[1:]:
            top_of = jnp.maximum(top_of, tile[:CHUNKS])
        scales = [jnp.exp(tile[:CHUNKS] - top_of) for tile in stats]
        total_of = sum(s * tile[CHUNKS:] for s, tile in zip(scales, stats))
        numers = []
        for c in range(CHUNKS):
            numer = first[:, chunk(c)] * scales[0][c:c + 1]
            for o in offsets:
                numer = numer + others[o, :, chunk(c)] * scales[o][c:c + 1]
            numers.append(numer)
        return top_of, total_of, numers

    arrive(get_c)
    compact = c_g[...].reshape(DH, BLOCK).astype(F32).T.astype(BF16)
    slot_col = jnp.concatenate(
        [jnp.broadcast_to(slots_ref[:, chunk(c)], (LANES, LANES)).T for c in range(CHUNKS)], axis=0
    )
    for c in range(CHUNKS):
        logits = dot(compact, queries[chunk(c), :], 1, 1) * INV_ROOT
        allowed = slot_col <= qp[c:c + 1, :]
        masked = jnp.where(allowed, logits, NEG_FILL)
        top = jnp.max(masked, axis=0, keepdims=True)
        raw = jnp.where(allowed, jnp.exp(masked - top), 0.0)
        feats[:, chunk(c)] = (raw * (1.0 / jnp.sum(raw, axis=0, keepdims=True))).astype(BF16)
    diagonal = lax.broadcasted_iota(jnp.int32, (LANES, LANES), 0) == lax.broadcasted_iota(jnp.int32, (LANES, LANES), 1)
    for i in range(CHUNKS):
        for j in range(i + 1):
            block = dot(feats[chunk(i), :], feats[chunk(j), :], 1, 1)
            gram[i, j] = block + jnp.where(diagonal, RIDGE, 0.0) if i == j else block

    def merge_z():
        arrive(get_s)
        arrive(get_n)
        top_z, total_z, numer_z = merge([s_z[o] for o in range(RING)], n_send.at[z], n_z)
        s_y[0] = jnp.concatenate([top_z, total_z], axis=0)
        for c in range(CHUNKS):
            n_y[0, :, chunk(c)] = numer_z[c]
        for o in offsets:
            copy_of(9, o, s_y.at[0], s_y.at[o], y_peer(o)).start()
            copy_of(10, o, n_y.at[0], n_y.at[o], y_peer(o)).start()

    def merge_y():
        for o in offsets:
            copy_of(9, o, s_y.at[0], s_y.at[o], y_peer(o)).wait()
            copy_of(10, o, n_y.at[0], n_y.at[o], y_peer(o)).wait()
        _, total, numer = merge([s_y[o] for o in range(RING)], n_y.at[0], n_y)
        for c in range(CHUNKS):
            o_g[z, :, chunk(c)] = (numer[c] / total[c:c + 1]).astype(BF16)
        for o in offsets:
            copy_of(11, o, o_g.at[z], o_g.at[z], z_peer(o)).start()

    def eliminate(b, carry):
        inverse[b] = invert_spd(gram[b, b])
        for c in range(CHUNKS - 1):
            @pl.when(b == c)
            def _():
                for i in range(c + 1, CHUNKS):
                    lower[i, c] = exact(gram[i, c], inverse[c], 1, 0)
                    upper[c, i] = exact(inverse[c], gram[i, c], 1, 1)
                for i in range(c + 1, CHUNKS):
                    for j in range(c + 1, i + 1):
                        gram[i, j] = gram[i, j] - exact(lower[i, c], gram[j, c], 1, 1)

        pl.when(b == MERGE_Z_AFTER)(merge_z)
        pl.when(b == MERGE_Y_AFTER)(merge_y)
        return carry

    lax.fori_loop(0, CHUNKS, eliminate, 0)

    for o in offsets:
        copy_of(11, o, o_g.at[z], o_g.at[z], z_peer(o)).wait()
    attended = o_g[...].reshape(DH, BLOCK)
    own_row = lax.broadcasted_iota(jnp.int32, (RING, BLOCK), 0) + me * RING
    pick = jnp.where(lax.broadcasted_iota(jnp.int32, (RING, BLOCK), 1) == own_row, 1.0, 0.0).astype(BF16)
    own_out[...] = dot(pick, attended, 1, 1).astype(BF16)
    cross = dot(feats[...], attended, 1, 1)
    part = []
    for i in range(CHUNKS):
        rhs = cross[chunk(i), :]
        for c in range(i):
            rhs = rhs - exact(lower[i, c], part[c], 1, 0)
        part.append(rhs)
    part = [exact(inverse[i], part[i], 1, 0) for i in range(CHUNKS)]
    for c in reversed(range(CHUNKS)):
        for i in range(c + 1, CHUNKS):
            part[c] = part[c] - exact(upper[c, i], part[i], 1, 0)
        fitted_ref[chunk(c), :] = part[c]
    for copy in started:
        copy.wait_send()


STREAMS = 12
MERGE_Z_AFTER = 0
MERGE_Y_AFTER = 2


def compaction(queries, qpos, keys, values, slots):
    vmem = pl.BlockSpec(memory_space=pltpu.VMEM)
    table = pltpu.VMEM((RING, SLAB, BLOCK), BF16)
    wide = pltpu.VMEM((RING, SLAB, BLOCK), F32)
    tile = pltpu.VMEM((RING, RING, LANES), F32)
    blocks = pltpu.VMEM((CHUNKS, CHUNKS, LANES, LANES), F32)
    return pl.pallas_call(
        compaction_kernel,
        out_shape=(
            jax.ShapeDtypeStruct((RING, DH), BF16),
            jax.ShapeDtypeStruct((BLOCK, DH), F32),
        ),
        in_specs=[pl.BlockSpec(memory_space=pl.ANY)] * 5,
        out_specs=(vmem,) * 2,
        scratch_shapes=[
            pltpu.SMEM((1, RING), jnp.int32),
            pltpu.VMEM((RING, DH), BF16),
            pltpu.VMEM((BLOCK, DH), BF16),
            pltpu.VMEM((BLOCK, DH), BF16),
            pltpu.VMEM((1, BLOCK), jnp.int32),
            pltpu.VMEM((RING, RING, DH), F32),
            pltpu.VMEM((RING, RING * RING, DH), BF16),
            pltpu.VMEM((RING, RING, LANES), jnp.int32),
            pltpu.VMEM((RING, RING, LANES), jnp.int32),
            table, table, table, table,
            pltpu.VMEM((DH, BLOCK), BF16),
            wide, wide, tile, wide, tile, table,
            pltpu.VMEM((BLOCK, BLOCK), BF16),
            blocks,
            pltpu.VMEM((CHUNKS, LANES, LANES), F32),
            blocks, blocks,
            pltpu.SemaphoreType.DMA((5,)),
            pltpu.SemaphoreType.DMA((STREAMS, RING)),
            pltpu.SemaphoreType.DMA((STREAMS, RING)),
        ],
        compiler_params=pltpu.CompilerParams(collective_id=0, has_side_effects=True),
        name="compaction",
    )(qpos, queries, keys, values, slots)


def shards(ref_queries, query_pos, cache_keys, cache_values, slot_index):
    own, fitted = compaction(ref_queries[0], query_pos, cache_keys[0], cache_values[0], slot_index)
    return (own[None], fitted[None])


def solution(mesh):
    in_specs = (
        P("head", "pos", None),
        P("head", "pos"),
        P("head", "pos", None),
        P("head", "pos", None),
        P("head", None),
    )
    out_specs = (P("head", "pos", None), P("head", None, None))
    return jax.shard_map(shards, mesh=mesh, in_specs=in_specs, out_specs=out_specs, check_vma=False)
```

```python
import math

import jax
import jax.numpy as jnp
from jax import lax
from jax.experimental import pallas as pl
from jax.experimental.pallas import tpu as pltpu
from jax.sharding import PartitionSpec as P

RIDGE = 1.0
NEG_FILL = -1e30
RING = 8
BLOCK = 512
DH = 128
LANES = 128
CHUNKS = BLOCK // LANES
SLAB = DH // RING
HALF = BLOCK // 2
QROWS = 4
INV_ROOT = 1.0 / math.sqrt(DH)
MESH_ID = pl.DeviceIdType.MESH
F32 = jnp.float32
BF16 = jnp.bfloat16


def dot(a, b, ca, cb, precision=None):
    return lax.dot_general(a, b, (((ca,), (cb,)), ((), ())), precision=precision, preferred_element_type=F32)


def chunk(c):
    return slice(c * LANES, (c + 1) * LANES)


def exact(a, b, ca, cb):
    return dot(a, b, ca, cb, lax.Precision.HIGHEST)


def tree_sum(terms):
    while len(terms) > 1:
        terms = [u + v for u, v in zip(terms[::2], terms[1::2])] + ([terms[-1]] if len(terms) % 2 else [])
    return terms[0]


def invert_spd(a):
    n = a.shape[0]
    sub = lax.broadcasted_iota(jnp.int32, (8, n), 0)
    lane = lax.broadcasted_iota(jnp.int32, (8, n), 1)

    def along(v, j):
        return jnp.broadcast_to(v[:, j:j + 1], (8, n))

    def down(v, i):
        return jnp.broadcast_to(v[i:i + 1, :], (8, n))

    rows = [a[8 * g:8 * g + 8, :] for g in range(n // 8)]
    unit, scaled = [], []
    for g0 in range(n // 8):
        k = 8 * g0
        m = [jnp.where(lane < n + j, along(rows[g0], k + j), 0.0) for j in range(8)]
        for t in range(0, 8, 2):
            p00, p10, p11 = down(m[t], t), down(m[t], t + 1), down(m[t + 1], t + 1)
            scale = 1.0 / (p00 * p11 - p10 * p10)
            i00, i11, i10 = p11 * scale, p00 * scale, -(p10 * scale)
            f0 = jnp.where(sub == t, -1.0, jnp.where(sub == t + 1, 0.0, m[t]))
            f1 = jnp.where(sub == t + 1, -1.0, jnp.where(sub == t, 0.0, m[t + 1]))
            pivots = (sub == t) | (sub == t + 1)
            new = []
            for j in range(8):
                if j == t:
                    new.append(-(f0 * i00 + f1 * i10))
                elif j == t + 1:
                    new.append(-(f0 * i10 + f1 * i11))
                else:
                    w0, w1 = down(m[j], t), down(m[j], t + 1)
                    x0, x1 = i00 * w0 + i10 * w1, i10 * w0 + i11 * w1
                    new.append(jnp.where(pivots, 0.0, m[j]) - (f0 * x0 + f1 * x1))
            m = new
        own = (lane >= k) & (lane < k + 8)
        w = jnp.where(own, jnp.where(lane - k == sub, 1.0, 0.0), rows[g0])
        x = tree_sum([m[j] * down(w, j) for j in range(8)])
        unit.append(jnp.where(lane < k + 8, w, 0.0))
        scaled.append(jnp.where(lane < k + 8, x, 0.0))
        if k + 8 < n:
            xs = [down(x, j) for j in range(8)]
        for g in range(g0 + 1, n // 8):
            rows[g] = jnp.where(own, 0.0, rows[g]) - tree_sum([along(rows[g], k + j) * xs[j] for j in range(8)])
    return exact(jnp.concatenate(unit, axis=0), jnp.concatenate(scaled, axis=0), 0, 0)


def compaction_kernel(
    qpos_hbm, q_hbm, k_hbm, v_hbm, slots_hbm,
    own_out, fitted_ref,
    qpos_ref, q_ref, k_ref, v_ref, slots_ref,
    q_1, q_2, qp_1, qp_2, c_0, c_1, c_2, c_3, vt, n_0, n_1, s_1, n_2, s_2, o_3, feats,
    load_sems, send_sems, recv_sems,
):
    me = lax.axis_index("pos")
    place = (lax.div(me, RING), lax.rem(me, RING))

    def peer(axis, o):
        if axis == 0:
            return {"pos": lax.rem(place[0] + o, RING) * RING + place[1]}
        return {"pos": place[0] * RING + lax.rem(place[1] + o, RING)}

    offsets = (4, 3, 5, 2, 6, 1, 7)
    barrier = pltpu.get_barrier_semaphore()
    for axis in (0, 1):
        for o in offsets:
            pl.semaphore_signal(barrier, inc=1, device_id=peer(axis, o), device_id_type=MESH_ID)

    loads = [
        pltpu.make_async_copy(src, dst, load_sems.at[i])
        for i, (src, dst) in enumerate([
            (slots_hbm, slots_ref), (k_hbm, k_ref), (qpos_hbm, qpos_ref), (q_hbm, q_ref), (v_hbm, v_ref),
        ])
    ]
    for load in loads:
        load.start()
    for load in loads[:4]:
        load.wait()

    started = []

    def send(stream, axis, o, src, dst):
        copy = pltpu.make_async_remote_copy(
            src_ref=src, dst_ref=dst, send_sem=send_sems.at[stream, o], recv_sem=recv_sems.at[stream, o],
            device_id=peer(axis, o), device_id_type=MESH_ID,
        )
        copy.start()
        started.append(copy)
        return copy

    def arrive(copies):
        for copy in copies:
            copy.wait_recv()

    halves = (0, 1)

    base = me * BLOCK
    lane_id = (
        lax.broadcasted_iota(jnp.int32, (CHUNKS, LANES), 0) * LANES
        + lax.broadcasted_iota(jnp.int32, (CHUNKS, LANES), 1)
    )
    own_id = [
        HALF * h + place[h] * (RING * QROWS) + place[1 - h] * QROWS + i for h in halves for i in range(QROWS)
    ]
    tile = jnp.zeros((CHUNKS, LANES), jnp.int32)
    for i in range(RING):
        tile = jnp.where(lane_id == own_id[i], qpos_ref[0, i], tile)
    qp_1[0] = tile
    own_q = q_ref[...].astype(F32)
    for h in halves:
        q_1[h, place[1 - h]] = own_q[QROWS * h:QROWS * h + QROWS, :]
    position = lax.broadcasted_iota(jnp.int32, (BLOCK, BLOCK), 0) + base
    one_hot = jnp.where(position == slots_ref[...], 1.0, 0.0).astype(BF16)
    picked = dot(k_ref[...], one_hot, 0, 0).astype(BF16)
    for h in halves:
        c_0[h] = picked[:, h * HALF:(h + 1) * HALF].reshape(RING, SLAB, HALF)

    pl.semaphore_wait(barrier, 2 * (RING - 1))

    get_q = [send(h, 1 - h, o, q_1.at[h, place[1 - h]], q_1.at[h, place[1 - h]]) for h in halves for o in offsets]
    get_qp = [send(2, 1, o, qp_1.at[0], qp_1.at[o]) for o in offsets]
    get_c = [send(3 + h, h, o, c_0.at[h, lax.rem(place[h] + o, RING)], c_1.at[h, o]) for o in offsets for h in halves]
    loads[4].wait()
    vt[...] = v_ref[...].astype(F32).T.astype(BF16)

    arrive(get_q)
    for h in halves:
        q_2[h, place[h]] = q_1[h].reshape(RING * QROWS, DH).astype(BF16)
    get_q = [send(5 + h, h, o, q_2.at[h, place[h]], q_2.at[h, place[h]]) for o in offsets for h in halves]
    arrive(get_qp)
    qp_2[0] = tree_sum([qp_1[o] for o in range(RING)])
    get_qp = [send(7, 0, o, qp_2.at[0], qp_2.at[o]) for o in offsets]

    arrive(get_c)
    for h in halves:
        c_2[h, 0] = tree_sum([c_0[h, place[h]].astype(F32)] + [c_1[h, o].astype(F32) for o in offsets]).astype(BF16)
    get_c = [send(8 + h, 1 - h, o, c_2.at[h, 0], c_2.at[h, o]) for o in offsets for h in halves]

    arrive(get_q)
    arrive(get_qp)
    qp = tree_sum([qp_2[o] for o in range(RING)])
    queries = q_2[...].reshape(BLOCK, DH)

    arrive(get_c)
    for h in halves:
        c_3[h, place[h]] = tree_sum([c_2[h, o].astype(F32) for o in range(RING)]).astype(BF16)
    get_c = [send(10 + h, h, o, c_3.at[h, place[h]], c_3.at[h, place[h]]) for o in offsets for h in halves]

    key_pos = lax.broadcasted_iota(jnp.int32, (BLOCK, LANES), 0) + base
    get_s, get_n = [], []
    for h in halves:
        tops, totals = [], []
        for c in (0, 1):
            scores = dot(k_ref[...], queries[chunk(2 * h + c), :], 1, 1) * INV_ROOT
            allowed = key_pos <= qp[2 * h + c:2 * h + c + 1, :]
            masked = jnp.where(allowed, scores, NEG_FILL)
            top = jnp.max(masked, axis=0, keepdims=True)
            weights = jnp.where(allowed, jnp.exp(masked - top), 0.0)
            tops.append(top)
            totals.append(jnp.sum(weights, axis=0, keepdims=True))
            n_0[h, :, :, chunk(c)] = dot(vt[...], weights.astype(BF16), 1, 0).reshape(RING, SLAB, LANES)
        s_1[h, 0] = jnp.concatenate(tops + totals, axis=0)
    for o in offsets:
        for h in halves:
            get_s.append(send(12 + h, h, o, s_1.at[h, 0], s_1.at[h, o]))
            get_n.append(send(14 + h, h, o, n_0.at[h, lax.rem(place[h] + o, RING)], n_1.at[h, o]))

    def merge(stats, first, others, c):
        top = stats[0][c:c + 1]
        for tile in stats[1:]:
            top = jnp.maximum(top, tile[c:c + 1])
        scales = [jnp.exp(tile[c:c + 1] - top) for tile in stats]
        total = tree_sum([scale * tile[2 + c:3 + c] for scale, tile in zip(scales, stats)])
        numer = tree_sum(
            [first[:, chunk(c)] * scales[0]] + [others[o, :, chunk(c)] * scales[o] for o in range(1, RING)]
        )
        return top, total, numer

    arrive(get_c)
    compact = jnp.concatenate([c_3[h].reshape(DH, HALF).astype(F32).T for h in halves], axis=0).astype(BF16)
    slot_col = jnp.concatenate(
        [jnp.broadcast_to(slots_ref[:, chunk(c)], (LANES, LANES)).T for c in range(CHUNKS)], axis=0
    )
    for c in range(CHUNKS):
        logits = dot(compact, queries[chunk(c), :], 1, 1) * INV_ROOT
        allowed = slot_col <= qp[c:c + 1, :]
        masked = jnp.where(allowed, logits, NEG_FILL)
        top = jnp.max(masked, axis=0, keepdims=True)
        raw = jnp.where(allowed, jnp.exp(masked - top), 0.0)
        feats[:, chunk(c)] = (raw * (1.0 / jnp.sum(raw, axis=0, keepdims=True))).astype(BF16)
    diagonal = lax.broadcasted_iota(jnp.int32, (LANES, LANES), 0) == lax.broadcasted_iota(jnp.int32, (LANES, LANES), 1)
    gram = {}
    for i in range(CHUNKS):
        for j in range(i + 1):
            block = dot(feats[chunk(i), :], feats[chunk(j), :], 1, 1)
            gram[i, j] = block + jnp.where(diagonal, RIDGE, 0.0) if i == j else block

    def merge_first():
        for h in halves:
            merged = [merge([s_1[h, o] for o in range(RING)], n_0[h, place[h]], n_1[h], c) for c in (0, 1)]
            s_2[h, 0] = jnp.concatenate([m[0] for m in merged] + [m[1] for m in merged], axis=0)
            for c in (0, 1):
                n_2[h, 0, :, chunk(c)] = merged[c][2]
        return (
            [send(16 + h, 1 - h, o, s_2.at[h, 0], s_2.at[h, o]) for o in offsets for h in halves]
            + [send(18 + h, 1 - h, o, n_2.at[h, 0], n_2.at[h, o]) for o in offsets for h in halves]
        )

    def merge_second():
        for h in halves:
            for c in (0, 1):
                _, total, numer = merge([s_2[h, o] for o in range(RING)], n_2[h, 0], n_2[h], c)
                o_3[h, place[h], :, chunk(c)] = (numer / total).astype(BF16)
        return [send(20 + h, h, o, o_3.at[h, place[h]], o_3.at[h, place[h]]) for o in offsets for h in halves]

    inverse, lower, upper = {}, {}, {}

    def update(i, j, c):
        gram[i, j] = gram[i, j] - exact(lower[i, c], gram[j, c], 1, 1)

    def step(c):
        inverse[c] = invert_spd(gram[c, c])
        if c + 1 < CHUNKS:
            lower[c + 1, c] = exact(gram[c + 1, c], inverse[c], 1, 0)
            update(c + 1, c + 1, c)

    def rest(c):
        for i in range(c + 2, CHUNKS):
            lower[i, c] = exact(gram[i, c], inverse[c], 1, 0)
            for j in range(c + 1, i + 1):
                update(i, j, c)
        for i in range(c + 1, CHUNKS):
            upper[c, i] = exact(inverse[c], gram[i, c], 1, 1)

    arrive(get_s)
    arrive(get_n)
    get_n = merge_first()
    step(0)
    arrive(get_n)
    get_o = merge_second()
    rest(0)
    step(1)
    rest(1)
    step(2)
    arrive(get_o)
    attended = jnp.concatenate([o_3[h].reshape(DH, HALF) for h in halves], axis=1)
    row = lax.broadcasted_iota(jnp.int32, (RING, BLOCK), 0)
    column = lax.broadcasted_iota(jnp.int32, (RING, BLOCK), 1)
    pick = jnp.zeros((RING, BLOCK), F32)
    for i in range(RING):
        pick = jnp.where((row == i) & (column == own_id[i]), 1.0, pick)
    own_out[...] = dot(pick.astype(BF16), attended, 1, 1).astype(BF16)
    rest(2)
    part = [dot(feats[chunk(i), :], attended, 1, 1) for i in range(CHUNKS)]
    for c in range(CHUNKS - 1):
        for i in range(c + 1, CHUNKS):
            part[i] = part[i] - exact(lower[i, c], part[c], 1, 0)
    last = CHUNKS - 1
    share = {}
    for c in reversed(range(last)):
        part[c] = exact(inverse[c], part[c], 1, 0)
        share[c] = -upper[c, last]
        for i in range(c + 1, last):
            part[c] = part[c] - exact(upper[c, i], part[i], 1, 0)
            share[c] = share[c] - exact(upper[c, i], share[i], 1, 0)
    step(last)
    part[last] = exact(inverse[last], part[last], 1, 0)
    fitted_ref[chunk(last), :] = part[last]
    for c in range(last):
        fitted_ref[chunk(c), :] = part[c] + exact(share[c], part[last], 1, 0)
    for copy in started:
        copy.wait_send()


STREAMS = 22


def compaction(queries, qpos, keys, values, slots):
    vmem = pl.BlockSpec(memory_space=pltpu.VMEM)
    table = pltpu.VMEM((2, RING, SLAB, HALF), BF16)
    wide = pltpu.VMEM((2, RING, SLAB, HALF), F32)
    stats = pltpu.VMEM((2, RING, CHUNKS, LANES), F32)
    return pl.pallas_call(
        compaction_kernel,
        out_shape=(
            jax.ShapeDtypeStruct((RING, DH), BF16),
            jax.ShapeDtypeStruct((BLOCK, DH), F32),
        ),
        in_specs=[pl.BlockSpec(memory_space=pltpu.HBM)] * 5,
        out_specs=(vmem,) * 2,
        scratch_shapes=[
            pltpu.SMEM((1, RING), jnp.int32),
            pltpu.VMEM((RING, DH), BF16),
            pltpu.VMEM((BLOCK, DH), BF16),
            pltpu.VMEM((BLOCK, DH), BF16),
            pltpu.VMEM((1, BLOCK), jnp.int32),
            pltpu.VMEM((2, RING, QROWS, DH), F32),
            pltpu.VMEM((2, RING, RING * QROWS, DH), BF16),
            pltpu.VMEM((RING, CHUNKS, LANES), jnp.int32),
            pltpu.VMEM((RING, CHUNKS, LANES), jnp.int32),
            table, table, table, table,
            pltpu.VMEM((DH, BLOCK), BF16),
            wide, wide, stats, wide, stats, table,
            pltpu.VMEM((BLOCK, BLOCK), BF16),
            pltpu.SemaphoreType.DMA((5,)),
            pltpu.SemaphoreType.DMA((STREAMS, RING)),
            pltpu.SemaphoreType.DMA((STREAMS, RING)),
        ],
        compiler_params=pltpu.CompilerParams(collective_id=0, has_side_effects=True, vmem_limit_bytes=VMEM_LIMIT),
        name="compaction",
    )(qpos, queries, keys, values, slots)


VMEM_LIMIT = 32 * 1024 * 1024


def shards(ref_queries, query_pos, cache_keys, cache_values, slot_index):
    own, fitted = compaction(*(
        pltpu.with_memory_space_constraint(x, pltpu.HBM)
        for x in (ref_queries[0], query_pos, cache_keys[0], cache_values[0], slot_index)
    ))
    return (own[None], fitted[None])


def solution(mesh):
    in_specs = (
        P("head", "pos", None),
        P("head", "pos"),
        P("head", "pos", None),
        P("head", "pos", None),
        P("head", None),
    )
    out_specs = (P("head", "pos", None), P("head", None, None))
    return jax.shard_map(shards, mesh=mesh, in_specs=in_specs, out_specs=out_specs, check_vma=False)
```

```python
import functools
import math

import jax
import jax.numpy as jnp
from jax import lax
from jax.experimental import pallas as pl
from jax.experimental.pallas import tpu as pltpu
from jax.sharding import PartitionSpec as P

RIDGE = 1.0
NEG_FILL = -1e30
RING = 8
BLOCK = 512
DH = 128
LANES = 128
CHUNKS = BLOCK // LANES
SLAB = DH // RING
HALF = BLOCK // 2
QROWS = 4
INV_ROOT = 1.0 / math.sqrt(DH)
MESH_ID = pl.DeviceIdType.MESH
F32 = jnp.float32
BF16 = jnp.bfloat16


def dot(a, b, ca, cb, precision=None):
    return lax.dot_general(a, b, (((ca,), (cb,)), ((), ())), precision=precision, preferred_element_type=F32)


def chunk(c):
    return slice(c * LANES, (c + 1) * LANES)


def pieces(x):
    high = x.astype(BF16)
    rest = x - high.astype(F32)
    middle = rest.astype(BF16)
    return high, middle, (rest - middle.astype(F32)).astype(BF16)


def exact(a, b, ca, cb):
    ah, am, al = pieces(a)
    bh, bm, bl = pieces(b)

    def stacked(a0, b0, a1, b1):
        return dot(jnp.concatenate([a0, a1], axis=ca), jnp.concatenate([b0, b1], axis=cb), ca, cb)

    return stacked(ah, bl, al, bh) + stacked(ah, bm, am, bm) + stacked(ah, bh, am, bh)


def tree_sum(terms):
    while len(terms) > 1:
        terms = [u + v for u, v in zip(terms[::2], terms[1::2])] + ([terms[-1]] if len(terms) % 2 else [])
    return terms[0]


def invert_spd(a):
    n = a.shape[0]
    sub = lax.broadcasted_iota(jnp.int32, (8, n), 0)
    lane = lax.broadcasted_iota(jnp.int32, (8, n), 1)

    def along(v, j):
        return jnp.broadcast_to(v[:, j:j + 1], (8, n))

    def down(v, i):
        return jnp.broadcast_to(v[i:i + 1, :], (8, n))

    rows = [a[8 * g:8 * g + 8, :] for g in range(n // 8)]
    unit, scaled = [], []
    for g0 in range(n // 8):
        k = 8 * g0
        m = [jnp.where(lane < n + j, along(rows[g0], k + j), 0.0) for j in range(8)]
        for t in range(0, 8, 2):
            p00, p10, p11 = down(m[t], t), down(m[t], t + 1), down(m[t + 1], t + 1)
            scale = 1.0 / (p00 * p11 - p10 * p10)
            i00, i11, i10 = p11 * scale, p00 * scale, -(p10 * scale)
            f0 = jnp.where(sub == t, -1.0, jnp.where(sub == t + 1, 0.0, m[t]))
            f1 = jnp.where(sub == t + 1, -1.0, jnp.where(sub == t, 0.0, m[t + 1]))
            pivots = (sub == t) | (sub == t + 1)
            new = []
            for j in range(8):
                if j == t:
                    new.append(-(f0 * i00 + f1 * i10))
                elif j == t + 1:
                    new.append(-(f0 * i10 + f1 * i11))
                else:
                    w0, w1 = down(m[j], t), down(m[j], t + 1)
                    x0, x1 = i00 * w0 + i10 * w1, i10 * w0 + i11 * w1
                    new.append(jnp.where(pivots, 0.0, m[j]) - (f0 * x0 + f1 * x1))
            m = new
        own = (lane >= k) & (lane < k + 8)
        w = jnp.where(own, jnp.where(lane - k == sub, 1.0, 0.0), rows[g0])
        x = tree_sum([m[j] * down(w, j) for j in range(8)])
        unit.append(jnp.where(lane < k + 8, w, 0.0))
        scaled.append(jnp.where(lane < k + 8, x, 0.0))
        if k + 8 < n:
            xs = [down(x, j) for j in range(8)]
        copies = [[along(rows[g], k + j) for g in range(g0 + 1, n // 8)] for j in range(8)]
        for g in range(g0 + 1, n // 8):
            rows[g] = jnp.where(own, 0.0, rows[g]) - tree_sum([copies[j][g - g0 - 1] * xs[j] for j in range(8)])
    return exact(jnp.concatenate(unit, axis=0).T, jnp.concatenate(scaled, axis=0), 1, 0)


def compaction_kernel(
    qpos_hbm, q_hbm, k_hbm, v_hbm, slots_hbm,
    own_out, fitted_ref,
    qpos_ref, q_ref, k_ref, v_ref, slots_ref,
    q_1, q_2, qp_1, qp_2, c_0, c_1, c_2, c_3, vt, n_0, n_1, s_1, n_2, s_2, o_3, feats, gram, inverse, lower, upper, share, rest,
    load_sems, send_sems, recv_sems,
):
    me = lax.axis_index("pos")
    place = (lax.div(me, RING), lax.rem(me, RING))

    def peer(axis, o):
        if axis == 0:
            return {"pos": lax.rem(place[0] + o, RING) * RING + place[1]}
        return {"pos": place[0] * RING + lax.rem(place[1] + o, RING)}

    offsets = (4, 3, 5, 2, 6, 1, 7)
    barrier = pltpu.get_barrier_semaphore()
    for axis in (0, 1):
        for o in offsets:
            pl.semaphore_signal(barrier, inc=1, device_id=peer(axis, o), device_id_type=MESH_ID)

    loads = [
        pltpu.make_async_copy(src, dst, load_sems.at[i])
        for i, (src, dst) in enumerate([
            (slots_hbm, slots_ref), (k_hbm, k_ref), (qpos_hbm, qpos_ref), (q_hbm, q_ref), (v_hbm, v_ref),
        ])
    ]
    for load in loads:
        load.start()
    for load in loads[:4]:
        load.wait()

    def copy_of(stream, axis, o, src, dst):
        return pltpu.make_async_remote_copy(
            src_ref=src, dst_ref=dst, send_sem=send_sems.at[stream], recv_sem=recv_sems.at[stream],
            device_id=peer(axis, o), device_id_type=MESH_ID,
        )

    def all_of(stream, buffer):
        seven = buffer.at[pl.ds(0, RING - 1)]
        return copy_of(stream, 0, 1, seven, seven)

    def send_all(*streams):
        for o in offsets:
            for stream, axis, src_of, dst_of, _ in streams:
                copy_of(stream, axis, o, src_of(o), dst_of(o)).start()
        return [(stream, buffer) for stream, _, _, _, buffer in streams]

    def gather(stream, axis, buffer, slot):
        return (stream, axis, lambda o: buffer.at[slot], lambda o: buffer.at[slot], buffer)

    def spread(stream, axis, buffer):
        return (stream, axis, lambda o: buffer.at[0], lambda o: buffer.at[o], buffer)

    def scatter(stream, axis, source, buffer):
        return (
            stream, axis, lambda o: source.at[lax.rem(place[axis] + o, RING)], lambda o: buffer.at[o], buffer
        )

    def arrive(streams):
        for stream, buffer in streams:
            all_of(stream, buffer).wait_recv()

    halves = (0, 1)

    base = me * BLOCK
    lane_id = (
        lax.broadcasted_iota(jnp.int32, (CHUNKS, LANES), 0) * LANES
        + lax.broadcasted_iota(jnp.int32, (CHUNKS, LANES), 1)
    )
    own_id = [
        HALF * h + place[h] * (RING * QROWS) + place[1 - h] * QROWS + i for h in halves for i in range(QROWS)
    ]
    tile = jnp.zeros((CHUNKS, LANES), jnp.int32)
    for i in range(RING):
        tile = jnp.where(lane_id == own_id[i], qpos_ref[0, i], tile)
    qp_1[0] = tile
    own_q = q_ref[...].astype(F32)
    for h in halves:
        q_1[h, place[1 - h]] = own_q[QROWS * h:QROWS * h + QROWS, :]
    position = lax.broadcasted_iota(jnp.int32, (BLOCK, BLOCK), 0) + base
    one_hot = jnp.where(position == slots_ref[...], 1.0, 0.0).astype(BF16)
    picked = dot(k_ref[...], one_hot, 0, 0).astype(BF16)
    for h in halves:
        c_0[h] = picked[:, h * HALF:(h + 1) * HALF].reshape(RING, SLAB, HALF)

    pl.semaphore_wait(barrier, 2 * (RING - 1))

    get_q = send_all(*(gather(h, 1 - h, q_1.at[h], place[1 - h]) for h in halves))
    get_qp = send_all(spread(2, 1, qp_1))
    get_c = send_all(*(scatter(3 + h, h, c_0.at[h], c_1.at[h]) for h in halves))
    loads[4].wait()
    vt[...] = v_ref[...].astype(F32).T.astype(BF16)

    arrive(get_q)
    for h in halves:
        q_2[h, place[h]] = q_1[h].reshape(RING * QROWS, DH).astype(BF16)
    get_q = send_all(*(gather(5 + h, h, q_2.at[h], place[h]) for h in halves))
    arrive(get_qp)
    qp_2[0] = tree_sum([qp_1[o] for o in range(RING)])
    get_qp = send_all(spread(7, 0, qp_2))

    arrive(get_c)
    for h in halves:
        c_2[h, 0] = tree_sum([c_0[h, place[h]].astype(F32)] + [c_1[h, o].astype(F32) for o in offsets]).astype(BF16)
    get_c = send_all(*(spread(8 + h, 1 - h, c_2.at[h]) for h in halves))

    arrive(get_q)
    arrive(get_qp)
    qp = tree_sum([qp_2[o] for o in range(RING)])
    queries = q_2[...].reshape(BLOCK, DH)

    arrive(get_c)
    for h in halves:
        c_3[h, place[h]] = tree_sum([c_2[h, o].astype(F32) for o in range(RING)]).astype(BF16)
    get_c = send_all(*(gather(10 + h, h, c_3.at[h], place[h]) for h in halves))

    key_pos = lax.broadcasted_iota(jnp.int32, (BLOCK, LANES), 0) + base
    for h in halves:
        tops, totals = [], []
        for c in (0, 1):
            scores = dot(k_ref[...], queries[chunk(2 * h + c), :], 1, 1) * INV_ROOT
            allowed = key_pos <= qp[2 * h + c:2 * h + c + 1, :]
            masked = jnp.where(allowed, scores, NEG_FILL)
            top = jnp.max(masked, axis=0, keepdims=True)
            weights = jnp.where(allowed, jnp.exp(masked - top), 0.0)
            tops.append(top)
            totals.append(jnp.sum(weights, axis=0, keepdims=True))
            n_0[h, :, :, chunk(c)] = dot(vt[...], weights.astype(BF16), 1, 0).reshape(RING, SLAB, LANES)
        s_1[h, 0] = jnp.concatenate(tops + totals, axis=0)
    get_n = send_all(
        *(spread(12 + h, h, s_1.at[h]) for h in halves), *(scatter(14 + h, h, n_0.at[h], n_1.at[h]) for h in halves)
    )

    def merge(stats, first, others, c):
        top = stats[0][c:c + 1]
        for tile in stats[1:]:
            top = jnp.maximum(top, tile[c:c + 1])
        scales = [jnp.exp(tile[c:c + 1] - top) for tile in stats]
        total = tree_sum([scale * tile[2 + c:3 + c] for scale, tile in zip(scales, stats)])
        numer = tree_sum(
            [first[:, chunk(c)] * scales[0]] + [others[o, :, chunk(c)] * scales[o] for o in range(1, RING)]
        )
        return top, total, numer

    arrive(get_c)
    compact = jnp.concatenate([c_3[h].reshape(DH, HALF).astype(F32).T for h in halves], axis=0).astype(BF16)
    slot_col = jnp.concatenate(
        [jnp.broadcast_to(slots_ref[:, chunk(c)], (LANES, LANES)).T for c in range(CHUNKS)], axis=0
    )
    for c in range(CHUNKS):
        logits = dot(compact, queries[chunk(c), :], 1, 1) * INV_ROOT
        allowed = slot_col <= qp[c:c + 1, :]
        masked = jnp.where(allowed, logits, NEG_FILL)
        top = jnp.max(masked, axis=0, keepdims=True)
        raw = jnp.where(allowed, jnp.exp(masked - top), 0.0)
        feats[:, chunk(c)] = (raw * (1.0 / jnp.sum(raw, axis=0, keepdims=True))).astype(BF16)
    diagonal = lax.broadcasted_iota(jnp.int32, (LANES, LANES), 0) == lax.broadcasted_iota(jnp.int32, (LANES, LANES), 1)
    for i in range(CHUNKS):
        for j in range(i + 1):
            block = dot(feats[chunk(i), :], feats[chunk(j), :], 1, 1)
            gram[i, j] = block + jnp.where(diagonal, RIDGE, 0.0) if i == j else block

    def merge_first():
        for h in halves:
            merged = [merge([s_1[h, o] for o in range(RING)], n_0[h, place[h]], n_1[h], c) for c in (0, 1)]
            s_2[h, 0] = jnp.concatenate([m[0] for m in merged] + [m[1] for m in merged], axis=0)
            for c in (0, 1):
                n_2[h, 0, :, chunk(c)] = merged[c][2]
        send_all(
            *(spread(16 + h, 1 - h, s_2.at[h]) for h in halves), *(spread(18 + h, 1 - h, n_2.at[h]) for h in halves)
        )

    def merge_second():
        for h in halves:
            for c in (0, 1):
                _, total, numer = merge([s_2[h, o] for o in range(RING)], n_2[h, 0], n_2[h], c)
                o_3[h, place[h], :, chunk(c)] = (numer / total).astype(BF16)
        send_all(*(gather(20 + h, h, o_3.at[h], place[h]) for h in halves))

    arrive(get_n)
    merge_first()
    last = CHUNKS - 1

    def after(c):
        if c < last:
            for i in range(c + 1, CHUNKS):
                lower[i, c] = exact(gram[i, c], inverse[c], 1, 0)
                upper[c, i] = exact(inverse[c], gram[i, c], 1, 1)
            for i in range(c + 1, CHUNKS):
                for j in range(c + 1, i + 1):
                    gram[i, j] = gram[i, j] - exact(lower[i, c], gram[j, c], 1, 1)
        if c == MERGE_AFTER:
            arrive([(16 + h, s_2.at[h]) for h in halves] + [(18 + h, n_2.at[h]) for h in halves])
            merge_second()
        if c == last - 1:
            arrive([(20 + h, o_3.at[h]) for h in halves])
            attended = jnp.concatenate([o_3[h].reshape(DH, HALF) for h in halves], axis=1)
            row = lax.broadcasted_iota(jnp.int32, (RING, BLOCK), 0)
            column = lax.broadcasted_iota(jnp.int32, (RING, BLOCK), 1)
            pick = jnp.zeros((RING, BLOCK), F32)
            for i in range(RING):
                pick = jnp.where((row == i) & (column == own_id[i]), 1.0, pick)
            own_out[...] = dot(pick.astype(BF16), attended, 1, 1).astype(BF16)
            part = [dot(feats[chunk(i), :], attended, 1, 1) for i in range(CHUNKS)]
            for c in range(last):
                for i in range(c + 1, CHUNKS):
                    part[i] = part[i] - exact(lower[i, c], part[c], 1, 0)
            rest[...] = part[last]
            for c in reversed(range(last)):
                part[c] = exact(inverse[c], part[c], 1, 0)
                shared = -upper[c, last]
                for i in range(c + 1, last):
                    part[c] = part[c] - exact(upper[c, i], part[i], 1, 0)
                    shared = shared - exact(upper[c, i], share[i], 1, 0)
                share[c] = shared
                fitted_ref[chunk(c), :] = part[c]
            everything = [(2, qp_1), (7, qp_2)] + [
                (stream + h, buffer.at[h])
                for stream, buffer in [
                    (0, q_1), (3, c_1), (5, q_2), (8, c_2), (10, c_3), (12, s_1), (14, n_1), (16, s_2), (18, n_2), (20, o_3)
                ]
                for h in halves
            ]
            for stream, buffer in everything:
                all_of(stream, buffer).wait_send()
        if c == last:
            solved = exact(inverse[last], rest[...], 1, 0)
            fitted_ref[chunk(last), :] = solved
            for i in range(last):
                fitted_ref[chunk(i), :] = fitted_ref[chunk(i), :] + exact(share[i], solved, 1, 0)

    def eliminate(b, carry):
        inverse[b] = invert_spd(gram[b, b])
        for c in range(CHUNKS):
            pl.when(b == c)(functools.partial(after, c))
        return carry

    lax.fori_loop(0, CHUNKS, eliminate, 0)


MERGE_AFTER = 0
STREAMS = 22


def compaction(queries, qpos, keys, values, slots):
    vmem = pl.BlockSpec(memory_space=pltpu.VMEM)
    table = pltpu.VMEM((2, RING, SLAB, HALF), BF16)
    wide = pltpu.VMEM((2, RING, SLAB, HALF), F32)
    blocks = pltpu.VMEM((CHUNKS, CHUNKS, LANES, LANES), F32)
    stats = pltpu.VMEM((2, RING, CHUNKS, LANES), F32)
    return pl.pallas_call(
        compaction_kernel,
        out_shape=(
            jax.ShapeDtypeStruct((RING, DH), BF16),
            jax.ShapeDtypeStruct((BLOCK, DH), F32),
        ),
        in_specs=[pl.BlockSpec(memory_space=pltpu.HBM)] * 5,
        out_specs=(vmem,) * 2,
        scratch_shapes=[
            pltpu.SMEM((1, RING), jnp.int32),
            pltpu.VMEM((RING, DH), BF16),
            pltpu.VMEM((BLOCK, DH), BF16),
            pltpu.VMEM((BLOCK, DH), BF16),
            pltpu.VMEM((1, BLOCK), jnp.int32),
            pltpu.VMEM((2, RING, QROWS, DH), F32),
            pltpu.VMEM((2, RING, RING * QROWS, DH), BF16),
            pltpu.VMEM((RING, CHUNKS, LANES), jnp.int32),
            pltpu.VMEM((RING, CHUNKS, LANES), jnp.int32),
            table, table, table, table,
            pltpu.VMEM((DH, BLOCK), BF16),
            wide, wide, stats, wide, stats, table,
            pltpu.VMEM((BLOCK, BLOCK), BF16),
            blocks,
            pltpu.VMEM((CHUNKS, LANES, LANES), F32),
            blocks, blocks,
            pltpu.VMEM((CHUNKS, LANES, LANES), F32),
            pltpu.VMEM((LANES, DH), F32),
            pltpu.SemaphoreType.DMA((5,)),
            pltpu.SemaphoreType.DMA((STREAMS,)),
            pltpu.SemaphoreType.DMA((STREAMS,)),
        ],
        compiler_params=pltpu.CompilerParams(collective_id=0, has_side_effects=True, vmem_limit_bytes=VMEM_LIMIT),
        name="compaction",
    )(qpos, queries, keys, values, slots)


VMEM_LIMIT = 32 * 1024 * 1024


def shards(ref_queries, query_pos, cache_keys, cache_values, slot_index):
    own, fitted = compaction(*(
        pltpu.with_memory_space_constraint(x, pltpu.HBM)
        for x in (ref_queries[0], query_pos, cache_keys[0], cache_values[0], slot_index)
    ))
    return (own[None], fitted[None])


def solution(mesh):
    in_specs = (
        P("head", "pos", None),
        P("head", "pos"),
        P("head", "pos", None),
        P("head", "pos", None),
        P("head", None),
    )
    out_specs = (P("head", "pos", None), P("head", None, None))
    return jax.shard_map(shards, mesh=mesh, in_specs=in_specs, out_specs=out_specs, check_vma=False)
```

```python
import functools
import math

import jax
import jax.numpy as jnp
from jax import lax
from jax.experimental import pallas as pl
from jax.experimental.pallas import tpu as pltpu
from jax.sharding import PartitionSpec as P

RIDGE = 1.0
NEG_FILL = -1e30
RING = 8
BLOCK = 512
DH = 128
LANES = 128
CHUNKS = BLOCK // LANES
SLAB = DH // RING
HALF = BLOCK // 2
QROWS = 4
INV_ROOT = 1.0 / math.sqrt(DH)
MESH_ID = pl.DeviceIdType.MESH
F32 = jnp.float32
BF16 = jnp.bfloat16


def dot(a, b, ca, cb, precision=None):
    return lax.dot_general(a, b, (((ca,), (cb,)), ((), ())), precision=precision, preferred_element_type=F32)


def chunk(c):
    return slice(c * LANES, (c + 1) * LANES)


def pieces(x):
    high = x.astype(BF16)
    rest = x - high.astype(F32)
    middle = rest.astype(BF16)
    return high, middle, (rest - middle.astype(F32)).astype(BF16)


def stacked(ca, cb, *pairs):
    return dot(
        jnp.concatenate([a for a, _ in pairs], axis=ca), jnp.concatenate([b for _, b in pairs], axis=cb), ca, cb
    )


def exact(a, b, ca, cb):
    ah, am, al = pieces(a)
    bh, bm, bl = pieces(b)
    small = stacked(ca, cb, (ah, bl), (al, bh))
    return small + stacked(ca, cb, (ah, bm), (am, bm)) + stacked(ca, cb, (ah, bh), (am, bh))


def close(pairs):
    split = [(pieces(a), pieces(b)) for a, b in pairs]
    cross_terms = [term for (ah, am, _), (bh, bm, _) in split for term in ((ah, bm), (am, bh))]
    return stacked(1, 0, *cross_terms) + stacked(1, 0, *[(a[0], b[0]) for a, b in split])


def tree_sum(terms):
    while len(terms) > 1:
        terms = [u + v for u, v in zip(terms[::2], terms[1::2])] + ([terms[-1]] if len(terms) % 2 else [])
    return terms[0]


def invert_spd(a):
    n = a.shape[0]
    sub = lax.broadcasted_iota(jnp.int32, (8, n), 0)
    lane = lax.broadcasted_iota(jnp.int32, (8, n), 1)

    def along(v, j):
        return jnp.broadcast_to(v[:, j:j + 1], (8, n))

    def down(v, i):
        return jnp.broadcast_to(v[i:i + 1, :], (8, n))

    def kept(v):
        return [jnp.where(lane < n + j, u, 0.0) for j, u in enumerate(v)]

    def invert_pivot(m):
        for t in range(0, 8, 2):
            p00, p10, p11 = down(m[t], t), down(m[t], t + 1), down(m[t + 1], t + 1)
            scale = 1.0 / (p00 * p11 - p10 * p10)
            i00, i11, i10 = p11 * scale, p00 * scale, -(p10 * scale)
            f0 = jnp.where(sub == t, -1.0, jnp.where(sub == t + 1, 0.0, m[t]))
            f1 = jnp.where(sub == t + 1, -1.0, jnp.where(sub == t, 0.0, m[t + 1]))
            pivots = (sub == t) | (sub == t + 1)
            new = []
            for j in range(8):
                if j == t:
                    new.append(-(f0 * i00 + f1 * i10))
                elif j == t + 1:
                    new.append(-(f0 * i10 + f1 * i11))
                else:
                    w0, w1 = down(m[j], t), down(m[j], t + 1)
                    x0, x1 = i00 * w0 + i10 * w1, i10 * w0 + i11 * w1
                    new.append(jnp.where(pivots, 0.0, m[j]) - (f0 * x0 + f1 * x1))
            m = new
        return m

    rows = [a[8 * g:8 * g + 8, :] for g in range(n // 8)]
    middle = n // 16
    unit, scaled, unit_half, scaled_half = [], [], [], []

    def solve_row(g, inverted):
        k = 8 * g
        w = jnp.where((lane >= k) & (lane < k + 8), jnp.where(lane - k == sub, 1.0, 0.0), rows[g])
        x = tree_sum([inverted[j] * down(w, j) for j in range(8)])
        unit.append(jnp.where(lane < k + 8, w, 0.0))
        scaled.append(jnp.where(lane < k + 8, x, 0.0))
        if g < middle:
            unit_half.append(w)
            scaled_half.append(jnp.where((lane < k + 8) | (lane >= n // 2), x, 0.0))
        return [down(x, j) for j in range(8)]

    def eliminate_row(g, of, factors, xs):
        k = 8 * of
        own = (lane >= k) & (lane < k + 8)
        rows[g] = jnp.where(own, 0.0, rows[g]) - tree_sum([factors[j] * xs[j] for j in range(8)])

    for g0 in range(0, n // 8, 2):
        if g0 == middle:
            share = exact(jnp.concatenate(unit_half, axis=0).T[n // 2:, :], jnp.concatenate(scaled_half, axis=0), 1, 0)
            for g in range(middle, n // 8):
                rows[g] = jnp.where(lane < n // 2, 0.0, rows[g]) - share[8 * (g - middle):8 * (g - middle) + 8, :]
        g1 = g0 + 1
        m = kept([along(rows[g0], 8 * g0 + j) for j in range(8)])
        b = kept([along(rows[g1], 8 * g0 + j) for j in range(8)])
        m1 = [along(rows[g1], 8 * g1 + j) for j in range(8)]
        later = range(g0 + 2, middle if g0 < middle else n // 8)
        factors = {g: [along(rows[g], 8 * g0 + j) for j in range(8)] for g in later}
        m = invert_pivot(m)
        bm = [tree_sum([b[i] * down(m[j], i) for i in range(8)]) for j in range(8)]
        m1 = [m1[j] - tree_sum([bm[i] * down(b[i], j) for i in range(8)]) for j in range(8)]
        xs = solve_row(g0, m)
        eliminate_row(g1, g0, b, xs)
        for g in later:
            eliminate_row(g, g0, factors[g], xs)
        factors = {g: [along(rows[g], 8 * g1 + j) for j in range(8)] for g in later}
        m1 = invert_pivot(m1)
        xs = solve_row(g1, m1)
        for g in later:
            eliminate_row(g, g1, factors[g], xs)
    return exact(jnp.concatenate(unit, axis=0).T, jnp.concatenate(scaled, axis=0), 1, 0)


def compaction_kernel(
    qpos_hbm, q_hbm, k_hbm, v_hbm, slots_hbm,
    own_out, fitted_ref,
    qpos_ref, q_ref, k_ref, v_ref, slots_ref,
    q_1, q_2, qp_1, qp_2, c_0, c_1, c_2, c_3, vt, n_0, n_1, s_1, n_2, s_2, o_3, feats, gram, inverse, lower, upper, share, rest,
    load_sems, send_sems, recv_sems,
):
    me = lax.axis_index("pos")
    place = (lax.div(me, RING), lax.rem(me, RING))

    def peer(axis, o):
        if axis == 0:
            return {"pos": lax.rem(place[0] + o, RING) * RING + place[1]}
        return {"pos": place[0] * RING + lax.rem(place[1] + o, RING)}

    offsets = (4, 3, 5, 2, 6, 1, 7)
    barrier = pltpu.get_barrier_semaphore()
    for axis in (0, 1):
        for o in offsets:
            pl.semaphore_signal(barrier, inc=1, device_id=peer(axis, o), device_id_type=MESH_ID)

    loads = [
        pltpu.make_async_copy(src, dst, load_sems.at[i])
        for i, (src, dst) in enumerate([
            (slots_hbm, slots_ref), (k_hbm, k_ref), (qpos_hbm, qpos_ref), (q_hbm, q_ref), (v_hbm, v_ref),
        ])
    ]
    for load in loads:
        load.start()
    for load in loads[:4]:
        load.wait()

    def copy_of(stream, axis, o, src, dst):
        return pltpu.make_async_remote_copy(
            src_ref=src, dst_ref=dst, send_sem=send_sems.at[stream], recv_sem=recv_sems.at[stream],
            device_id=peer(axis, o), device_id_type=MESH_ID,
        )

    def all_of(stream, buffer):
        seven = buffer.at[pl.ds(0, RING - 1)]
        return copy_of(stream, 0, 1, seven, seven)

    def send_all(*streams):
        for o in offsets:
            for stream, axis, src_of, dst_of, _ in streams:
                copy_of(stream, axis, o, src_of(o), dst_of(o)).start()
        return [(stream, buffer) for stream, _, _, _, buffer in streams]

    def gather(stream, axis, buffer, slot):
        return (stream, axis, lambda o: buffer.at[slot], lambda o: buffer.at[slot], buffer)

    def spread(stream, axis, buffer):
        return (stream, axis, lambda o: buffer.at[0], lambda o: buffer.at[o], buffer)

    def scatter(stream, axis, source, buffer):
        return (
            stream, axis, lambda o: source.at[lax.rem(place[axis] + o, RING)], lambda o: buffer.at[o], buffer
        )

    def arrive(streams):
        for stream, buffer in streams:
            all_of(stream, buffer).wait_recv()

    halves = (0, 1)

    base = me * BLOCK
    lane_id = (
        lax.broadcasted_iota(jnp.int32, (CHUNKS, LANES), 0) * LANES
        + lax.broadcasted_iota(jnp.int32, (CHUNKS, LANES), 1)
    )
    own_id = [
        HALF * h + place[h] * (RING * QROWS) + place[1 - h] * QROWS + i for h in halves for i in range(QROWS)
    ]
    tile = jnp.zeros((CHUNKS, LANES), jnp.int32)
    for i in range(RING):
        tile = jnp.where(lane_id == own_id[i], qpos_ref[0, i], tile)
    qp_1[0] = tile
    own_q = q_ref[...].astype(F32)
    for h in halves:
        q_1[h, place[1 - h]] = own_q[QROWS * h:QROWS * h + QROWS, :]
    position = lax.broadcasted_iota(jnp.int32, (BLOCK, BLOCK), 0) + base
    one_hot = jnp.where(position == slots_ref[...], 1.0, 0.0).astype(BF16)
    picked = dot(k_ref[...], one_hot, 0, 0).astype(BF16)
    for h in halves:
        c_0[h] = picked[:, h * HALF:(h + 1) * HALF].reshape(RING, SLAB, HALF)

    pl.semaphore_wait(barrier, 2 * (RING - 1))

    get_q = send_all(*(gather(h, 1 - h, q_1.at[h], place[1 - h]) for h in halves))
    get_qp = send_all(spread(2, 1, qp_1))
    get_c = send_all(*(scatter(3 + h, h, c_0.at[h], c_1.at[h]) for h in halves))
    loads[4].wait()
    vt[...] = v_ref[...].astype(F32).T.astype(BF16)

    arrive(get_q)
    for h in halves:
        q_2[h, place[h]] = q_1[h].reshape(RING * QROWS, DH).astype(BF16)
    get_q = send_all(*(gather(5 + h, h, q_2.at[h], place[h]) for h in halves))
    arrive(get_qp)
    qp_2[0] = tree_sum([qp_1[o] for o in range(RING)])
    get_qp = send_all(spread(7, 0, qp_2))

    arrive(get_c)
    for h in halves:
        c_2[h, 0] = tree_sum([c_0[h, place[h]].astype(F32)] + [c_1[h, o].astype(F32) for o in offsets]).astype(BF16)
    get_c = send_all(*(spread(8 + h, 1 - h, c_2.at[h]) for h in halves))

    arrive(get_q)
    arrive(get_qp)
    qp = tree_sum([qp_2[o] for o in range(RING)])
    queries = q_2[...].reshape(BLOCK, DH)

    arrive(get_c)
    for h in halves:
        c_3[h, place[h]] = tree_sum([c_2[h, o].astype(F32) for o in range(RING)]).astype(BF16)
    get_c = send_all(*(gather(10 + h, h, c_3.at[h], place[h]) for h in halves))

    key_pos = lax.broadcasted_iota(jnp.int32, (BLOCK, LANES), 0) + base
    for h in halves:
        tops, totals = [], []
        for c in (0, 1):
            scores = dot(k_ref[...], queries[chunk(2 * h + c), :], 1, 1) * INV_ROOT
            allowed = key_pos <= qp[2 * h + c:2 * h + c + 1, :]
            masked = jnp.where(allowed, scores, NEG_FILL)
            top = jnp.max(masked, axis=0, keepdims=True)
            weights = jnp.where(allowed, jnp.exp(masked - top), 0.0)
            tops.append(top)
            totals.append(jnp.sum(weights, axis=0, keepdims=True))
            n_0[h, :, :, chunk(c)] = dot(vt[...], weights.astype(BF16), 1, 0).reshape(RING, SLAB, LANES)
        s_1[h, 0] = jnp.concatenate(tops + totals, axis=0)
    get_n = send_all(
        *(spread(12 + h, h, s_1.at[h]) for h in halves), *(scatter(14 + h, h, n_0.at[h], n_1.at[h]) for h in halves)
    )

    def merge(stats, first, others, c):
        top = stats[0][c:c + 1]
        for tile in stats[1:]:
            top = jnp.maximum(top, tile[c:c + 1])
        scales = [jnp.exp(tile[c:c + 1] - top) for tile in stats]
        total = tree_sum([scale * tile[2 + c:3 + c] for scale, tile in zip(scales, stats)])
        numer = tree_sum(
            [first[:, chunk(c)] * scales[0]] + [others[o, :, chunk(c)] * scales[o] for o in range(1, RING)]
        )
        return top, total, numer

    arrive(get_c)
    compact = jnp.concatenate([c_3[h].reshape(DH, HALF).astype(F32).T for h in halves], axis=0).astype(BF16)
    slot_col = jnp.concatenate(
        [jnp.broadcast_to(slots_ref[:, chunk(c)], (LANES, LANES)).T for c in range(CHUNKS)], axis=0
    )
    for c in range(CHUNKS):
        logits = dot(compact, queries[chunk(c), :], 1, 1) * INV_ROOT
        allowed = slot_col <= qp[c:c + 1, :]
        masked = jnp.where(allowed, logits, NEG_FILL)
        top = jnp.max(masked, axis=0, keepdims=True)
        raw = jnp.where(allowed, jnp.exp(masked - top), 0.0)
        feats[:, chunk(c)] = (raw * (1.0 / jnp.sum(raw, axis=0, keepdims=True))).astype(BF16)
    diagonal = lax.broadcasted_iota(jnp.int32, (LANES, LANES), 0) == lax.broadcasted_iota(jnp.int32, (LANES, LANES), 1)
    for i in range(CHUNKS):
        for j in range(i + 1):
            block = dot(feats[chunk(i), :], feats[chunk(j), :], 1, 1)
            gram[i, j] = block + jnp.where(diagonal, RIDGE, 0.0) if i == j else block

    def merge_first():
        for h in halves:
            merged = [merge([s_1[h, o] for o in range(RING)], n_0[h, place[h]], n_1[h], c) for c in (0, 1)]
            s_2[h, 0] = jnp.concatenate([m[0] for m in merged] + [m[1] for m in merged], axis=0)
            for c in (0, 1):
                n_2[h, 0, :, chunk(c)] = merged[c][2]
        send_all(
            *(spread(16 + h, 1 - h, s_2.at[h]) for h in halves), *(spread(18 + h, 1 - h, n_2.at[h]) for h in halves)
        )

    def merge_second():
        for h in halves:
            for c in (0, 1):
                _, total, numer = merge([s_2[h, o] for o in range(RING)], n_2[h, 0], n_2[h], c)
                o_3[h, place[h], :, chunk(c)] = (numer / total).astype(BF16)
        send_all(*(gather(20 + h, h, o_3.at[h], place[h]) for h in halves))

    arrive(get_n)
    merge_first()
    last = CHUNKS - 1

    def after(c):
        if c < last:
            for i in range(c + 1, CHUNKS):
                lower[i, c] = exact(gram[i, c], inverse[c], 1, 0)
                upper[c, i] = exact(inverse[c], gram[i, c], 1, 1)
            for i in range(c + 1, CHUNKS):
                for j in range(c + 1, i + 1):
                    gram[i, j] = gram[i, j] - exact(lower[i, c], gram[j, c], 1, 1)
        if c == MERGE_AFTER:
            arrive([(16 + h, s_2.at[h]) for h in halves] + [(18 + h, n_2.at[h]) for h in halves])
            merge_second()
        if c == last - 1:
            arrive([(20 + h, o_3.at[h]) for h in halves])
            attended = jnp.concatenate([o_3[h].reshape(DH, HALF) for h in halves], axis=1)
            row = lax.broadcasted_iota(jnp.int32, (RING, BLOCK), 0)
            column = lax.broadcasted_iota(jnp.int32, (RING, BLOCK), 1)
            pick = jnp.zeros((RING, BLOCK), F32)
            for i in range(RING):
                pick = jnp.where((row == i) & (column == own_id[i]), 1.0, pick)
            own_out[...] = dot(pick.astype(BF16), attended, 1, 1).astype(BF16)
            part = [dot(feats[chunk(i), :], attended, 1, 1) for i in range(CHUNKS)]
            for i in range(1, CHUNKS):
                part[i] = part[i] - close([(lower[i, j], part[j]) for j in range(i)])
            rest[...] = part[last]
            for i in reversed(range(last)):
                part[i] = jnp.concatenate([close([(inverse[i], part[i])]), -upper[i, last]], axis=1)
                if i + 1 < last:
                    part[i] = part[i] - close([(upper[i, j], part[j]) for j in range(i + 1, last)])
                fitted_ref[chunk(i), :] = part[i][:, :DH]
                share[i] = part[i][:, DH:]
            everything = [(2, qp_1), (7, qp_2)] + [
                (stream + h, buffer.at[h])
                for stream, buffer in [
                    (0, q_1), (3, c_1), (5, q_2), (8, c_2), (10, c_3), (12, s_1), (14, n_1), (16, s_2), (18, n_2), (20, o_3)
                ]
                for h in halves
            ]
            for stream, buffer in everything:
                all_of(stream, buffer).wait_send()
        if c == last:
            solved = close([(inverse[last], rest[...])])
            fitted_ref[chunk(last), :] = solved
            for i in range(last):
                fitted_ref[chunk(i), :] = fitted_ref[chunk(i), :] + close([(share[i], solved)])

    def eliminate(b, carry):
        inverse[b] = invert_spd(gram[b, b])
        for c in range(CHUNKS):
            pl.when(b == c)(functools.partial(after, c))
        return carry

    lax.fori_loop(0, CHUNKS, eliminate, 0)


MERGE_AFTER = 0
STREAMS = 22


def compaction(queries, qpos, keys, values, slots):
    vmem = pl.BlockSpec(memory_space=pltpu.VMEM)
    table = pltpu.VMEM((2, RING, SLAB, HALF), BF16)
    wide = pltpu.VMEM((2, RING, SLAB, HALF), F32)
    blocks = pltpu.VMEM((CHUNKS, CHUNKS, LANES, LANES), F32)
    stats = pltpu.VMEM((2, RING, CHUNKS, LANES), F32)
    return pl.pallas_call(
        compaction_kernel,
        out_shape=(
            jax.ShapeDtypeStruct((RING, DH), BF16),
            jax.ShapeDtypeStruct((BLOCK, DH), F32),
        ),
        in_specs=[pl.BlockSpec(memory_space=pltpu.HBM)] * 5,
        out_specs=(vmem,) * 2,
        scratch_shapes=[
            pltpu.SMEM((1, RING), jnp.int32),
            pltpu.VMEM((RING, DH), BF16),
            pltpu.VMEM((BLOCK, DH), BF16),
            pltpu.VMEM((BLOCK, DH), BF16),
            pltpu.VMEM((1, BLOCK), jnp.int32),
            pltpu.VMEM((2, RING, QROWS, DH), F32),
            pltpu.VMEM((2, RING, RING * QROWS, DH), BF16),
            pltpu.VMEM((RING, CHUNKS, LANES), jnp.int32),
            pltpu.VMEM((RING, CHUNKS, LANES), jnp.int32),
            table, table, table, table,
            pltpu.VMEM((DH, BLOCK), BF16),
            wide, wide, stats, wide, stats, table,
            pltpu.VMEM((BLOCK, BLOCK), BF16),
            blocks,
            pltpu.VMEM((CHUNKS, LANES, LANES), F32),
            blocks, blocks,
            pltpu.VMEM((CHUNKS, LANES, LANES), F32),
            pltpu.VMEM((LANES, DH), F32),
            pltpu.SemaphoreType.DMA((5,)),
            pltpu.SemaphoreType.DMA((STREAMS,)),
            pltpu.SemaphoreType.DMA((STREAMS,)),
        ],
        compiler_params=pltpu.CompilerParams(collective_id=0, has_side_effects=True, vmem_limit_bytes=VMEM_LIMIT),
        name="compaction",
    )(qpos, queries, keys, values, slots)


VMEM_LIMIT = 32 * 1024 * 1024


def emit_kernel(own_ref, fitted_ref, own_out, fitted_out):
    own_out[0] = own_ref[...]
    fitted_out[0] = fitted_ref[...]


def emit(own, fitted):
    vmem = pl.BlockSpec(memory_space=pltpu.VMEM)
    return pl.pallas_call(
        emit_kernel,
        out_shape=(
            jax.ShapeDtypeStruct((1, RING, DH), BF16),
            jax.ShapeDtypeStruct((1, BLOCK, DH), F32),
        ),
        in_specs=[vmem] * 2,
        out_specs=(vmem,) * 2,
        compiler_params=pltpu.CompilerParams(vmem_limit_bytes=VMEM_LIMIT),
        name="emit",
    )(own, fitted)


def shards(ref_queries, query_pos, cache_keys, cache_values, slot_index):
    own, fitted = compaction(*(
        pltpu.with_memory_space_constraint(x, pltpu.HBM)
        for x in (ref_queries[0], query_pos, cache_keys[0], cache_values[0], slot_index)
    ))
    return emit(own, fitted)


def solution(mesh):
    in_specs = (
        P("head", "pos", None),
        P("head", "pos"),
        P("head", "pos", None),
        P("head", "pos", None),
        P("head", None),
    )
    out_specs = (P("head", "pos", None), P("head", None, None))
    return jax.shard_map(shards, mesh=mesh, in_specs=in_specs, out_specs=out_specs, check_vma=False)
```

```python
import functools
import math

import jax
import jax.numpy as jnp
from jax import lax
from jax.experimental import pallas as pl
from jax.experimental.pallas import tpu as pltpu
from jax.sharding import PartitionSpec as P

RIDGE = 1.0
NEG_FILL = -1e30
RING = 8
BLOCK = 512
DH = 128
LANES = 128
CHUNKS = BLOCK // LANES
SLAB = DH // RING
HALF = BLOCK // 2
QROWS = 4
INV_ROOT = 1.0 / math.sqrt(DH)
MESH_ID = pl.DeviceIdType.MESH
F32 = jnp.float32
BF16 = jnp.bfloat16


def dot(a, b, ca, cb, precision=None):
    return lax.dot_general(a, b, (((ca,), (cb,)), ((), ())), precision=precision, preferred_element_type=F32)


def chunk(c):
    return slice(c * LANES, (c + 1) * LANES)


def pieces(x):
    high = x.astype(BF16)
    rest = x - high.astype(F32)
    middle = rest.astype(BF16)
    return high, middle, (rest - middle.astype(F32)).astype(BF16)


def stacked(ca, cb, *pairs):
    return dot(
        jnp.concatenate([a for a, _ in pairs], axis=ca), jnp.concatenate([b for _, b in pairs], axis=cb), ca, cb
    )


def exact(a, b, ca, cb):
    ah, am, al = pieces(a)
    bh, bm, bl = pieces(b)
    small = stacked(ca, cb, (ah, bl), (al, bh))
    return small + stacked(ca, cb, (ah, bm), (am, bm)) + stacked(ca, cb, (ah, bh), (am, bh))


def close(pairs):
    split = [(pieces(a), pieces(b)) for a, b in pairs]
    cross_terms = [term for (ah, am, _), (bh, bm, _) in split for term in ((ah, bm), (am, bh))]
    return stacked(1, 0, *cross_terms) + stacked(1, 0, *[(a[0], b[0]) for a, b in split])


def tree_sum(terms):
    while len(terms) > 1:
        terms = [u + v for u, v in zip(terms[::2], terms[1::2])] + ([terms[-1]] if len(terms) % 2 else [])
    return terms[0]


def factor_spd(a, halfway):
    n = a.shape[0]
    sub = lax.broadcasted_iota(jnp.int32, (8, n), 0)
    lane = lax.broadcasted_iota(jnp.int32, (8, n), 1)

    def along(v, j):
        return jnp.broadcast_to(v[:, j:j + 1], (8, n))

    def down(v, i):
        return jnp.broadcast_to(v[i:i + 1, :], (8, n))

    def kept(v):
        return [jnp.where(lane < n + j, u, 0.0) for j, u in enumerate(v)]

    def invert_pivot(m):
        for t in range(0, 8, 2):
            p00, p10, p11 = down(m[t], t), down(m[t], t + 1), down(m[t + 1], t + 1)
            scale = 1.0 / (p00 * p11 - p10 * p10)
            i00, i11, i10 = p11 * scale, p00 * scale, -(p10 * scale)
            f0 = jnp.where(sub == t, -1.0, jnp.where(sub == t + 1, 0.0, m[t]))
            f1 = jnp.where(sub == t + 1, -1.0, jnp.where(sub == t, 0.0, m[t + 1]))
            pivots = (sub == t) | (sub == t + 1)
            new = []
            for j in range(8):
                if j == t:
                    new.append(-(f0 * i00 + f1 * i10))
                elif j == t + 1:
                    new.append(-(f0 * i10 + f1 * i11))
                else:
                    w0, w1 = down(m[j], t), down(m[j], t + 1)
                    x0, x1 = i00 * w0 + i10 * w1, i10 * w0 + i11 * w1
                    new.append(jnp.where(pivots, 0.0, m[j]) - (f0 * x0 + f1 * x1))
            m = new
        return m

    rows = [a[8 * g:8 * g + 8, :] for g in range(n // 8)]
    middle = n // 16
    unit, scaled, unit_half, scaled_half = [], [], [], []

    def solve_row(g, inverted):
        k = 8 * g
        w = jnp.where((lane >= k) & (lane < k + 8), jnp.where(lane - k == sub, 1.0, 0.0), rows[g])
        x = tree_sum([inverted[j] * down(w, j) for j in range(8)])
        unit.append(jnp.where(lane < k + 8, w, 0.0))
        scaled.append(jnp.where(lane < k + 8, x, 0.0))
        if g < middle:
            unit_half.append(w)
            scaled_half.append(jnp.where((lane < k + 8) | (lane >= n // 2), x, 0.0))
        return [down(x, j) for j in range(8)]

    def eliminate_row(g, of, factors, xs):
        k = 8 * of
        own = (lane >= k) & (lane < k + 8)
        rows[g] = jnp.where(own, 0.0, rows[g]) - tree_sum([factors[j] * xs[j] for j in range(8)])

    for g0 in range(0, n // 8, 2):
        if g0 == middle:
            halfway()
            share = exact(jnp.concatenate(unit_half, axis=0).T[n // 2:, :], jnp.concatenate(scaled_half, axis=0), 1, 0)
            for g in range(middle, n // 8):
                rows[g] = jnp.where(lane < n // 2, 0.0, rows[g]) - share[8 * (g - middle):8 * (g - middle) + 8, :]
        g1 = g0 + 1
        m = kept([along(rows[g0], 8 * g0 + j) for j in range(8)])
        b = kept([along(rows[g1], 8 * g0 + j) for j in range(8)])
        m1 = [along(rows[g1], 8 * g1 + j) for j in range(8)]
        later = range(g0 + 2, middle if g0 < middle else n // 8)
        factors = {g: [along(rows[g], 8 * g0 + j) for j in range(8)] for g in later}
        m = invert_pivot(m)
        bm = [tree_sum([b[i] * down(m[j], i) for i in range(8)]) for j in range(8)]
        m1 = [m1[j] - tree_sum([bm[i] * down(b[i], j) for i in range(8)]) for j in range(8)]
        xs = solve_row(g0, m)
        eliminate_row(g1, g0, b, xs)
        for g in later:
            eliminate_row(g, g0, factors[g], xs)
        factors = {g: [along(rows[g], 8 * g1 + j) for j in range(8)] for g in later}
        m1 = invert_pivot(m1)
        xs = solve_row(g1, m1)
        for g in later:
            eliminate_row(g, g1, factors[g], xs)
    return jnp.concatenate(unit, axis=0).T, jnp.concatenate(scaled, axis=0)


def compaction_kernel(
    qpos_hbm, q_hbm, k_hbm, v_hbm, slots_hbm,
    own_out, fitted_ref,
    qpos_ref, q_ref, k_ref, v_ref, slots_ref,
    q_1, q_2, qp_1, qp_2, c_0, c_1, c_2, c_3, vt, n_0, n_1, s_1, n_2, s_2, o_3, feats, gram, inverse, lower, upper, share, rest, unit, scaled,
    load_sems, send_sems, recv_sems,
):
    me = lax.axis_index("pos")
    place = (lax.div(me, RING), lax.rem(me, RING))

    def peer(axis, o):
        if axis == 0:
            return {"pos": lax.rem(place[0] + o, RING) * RING + place[1]}
        return {"pos": place[0] * RING + lax.rem(place[1] + o, RING)}

    offsets = (4, 3, 5, 2, 6, 1, 7)
    barrier = pltpu.get_barrier_semaphore()
    for o in offsets:
        for axis in (0, 1):
            pl.semaphore_signal(barrier, inc=1, device_id=peer(axis, o), device_id_type=MESH_ID)

    loads = [
        pltpu.make_async_copy(src, dst, load_sems.at[i])
        for i, (src, dst) in enumerate([
            (slots_hbm, slots_ref), (k_hbm, k_ref), (qpos_hbm, qpos_ref), (q_hbm, q_ref), (v_hbm, v_ref),
        ])
    ]
    for load in loads:
        load.start()
    for load in loads[:4]:
        load.wait()

    def copy_of(stream, axis, o, src, dst):
        return pltpu.make_async_remote_copy(
            src_ref=src, dst_ref=dst, send_sem=send_sems.at[stream], recv_sem=recv_sems.at[stream],
            device_id=peer(axis, o), device_id_type=MESH_ID,
        )

    def all_of(stream, buffer):
        seven = buffer.at[pl.ds(0, RING - 1)]
        return copy_of(stream, 0, 1, seven, seven)

    def send_all(*streams):
        for o in offsets:
            for stream, axis, src_of, dst_of, _ in streams:
                copy_of(stream, axis, o, src_of(o), dst_of(o)).start()
        return [(stream, buffer) for stream, _, _, _, buffer in streams]

    def gather(stream, axis, buffer, slot):
        return (stream, axis, lambda o: buffer.at[slot], lambda o: buffer.at[slot], buffer)

    def spread(stream, axis, buffer):
        return (stream, axis, lambda o: buffer.at[0], lambda o: buffer.at[o], buffer)

    def scatter(stream, axis, source, buffer):
        return (
            stream, axis, lambda o: source.at[lax.rem(place[axis] + o, RING)], lambda o: buffer.at[o], buffer
        )

    def arrive(streams):
        for stream, buffer in streams:
            all_of(stream, buffer).wait_recv()

    halves = (0, 1)

    base = me * BLOCK
    lane_id = (
        lax.broadcasted_iota(jnp.int32, (CHUNKS, LANES), 0) * LANES
        + lax.broadcasted_iota(jnp.int32, (CHUNKS, LANES), 1)
    )
    own_id = [
        HALF * h + place[h] * (RING * QROWS) + place[1 - h] * QROWS + i for h in halves for i in range(QROWS)
    ]
    tile = jnp.zeros((CHUNKS, LANES), jnp.int32)
    for i in range(RING):
        tile = jnp.where(lane_id == own_id[i], qpos_ref[0, i], tile)
    qp_1[0] = tile
    own_q = q_ref[...].astype(F32)
    for h in halves:
        q_1[h, place[1 - h]] = own_q[QROWS * h:QROWS * h + QROWS, :]
    position = lax.broadcasted_iota(jnp.int32, (BLOCK, BLOCK), 0) + base
    one_hot = jnp.where(position == slots_ref[...], 1.0, 0.0).astype(BF16)
    picked = dot(k_ref[...], one_hot, 0, 0).astype(BF16)
    for h in halves:
        c_0[h] = picked[:, h * HALF:(h + 1) * HALF].reshape(RING, SLAB, HALF)

    pl.semaphore_wait(barrier, 2 * (RING - 1))

    get_q = send_all(*(gather(h, 1 - h, q_1.at[h], place[1 - h]) for h in halves))
    get_qp = send_all(spread(2, 1, qp_1))
    get_c = send_all(*(scatter(3 + h, h, c_0.at[h], c_1.at[h]) for h in halves))
    loads[4].wait()
    vt[...] = v_ref[...].astype(F32).T.astype(BF16)

    arrive(get_q)
    for h in halves:
        q_2[h, place[h]] = q_1[h].reshape(RING * QROWS, DH).astype(BF16)
    get_q = send_all(*(gather(5 + h, h, q_2.at[h], place[h]) for h in halves))
    arrive(get_qp)
    qp_2[0] = tree_sum([qp_1[o] for o in range(RING)])
    get_qp = send_all(spread(7, 0, qp_2))

    arrive(get_c)
    for h in halves:
        c_2[h, 0] = tree_sum([c_0[h, place[h]].astype(F32)] + [c_1[h, o].astype(F32) for o in offsets]).astype(BF16)
    get_c = send_all(*(spread(8 + h, 1 - h, c_2.at[h]) for h in halves))

    arrive(get_q)
    arrive(get_qp)
    qp = tree_sum([qp_2[o] for o in range(RING)])
    queries = q_2[...].reshape(BLOCK, DH)

    arrive(get_c)
    for h in halves:
        c_3[h, place[h]] = tree_sum([c_2[h, o].astype(F32) for o in range(RING)]).astype(BF16)
    get_c = send_all(*(gather(10 + h, h, c_3.at[h], place[h]) for h in halves))

    key_pos = lax.broadcasted_iota(jnp.int32, (BLOCK, LANES), 0) + base
    for h in halves:
        tops, totals = [], []
        for c in (0, 1):
            scores = dot(k_ref[...], queries[chunk(2 * h + c), :], 1, 1) * INV_ROOT
            allowed = key_pos <= qp[2 * h + c:2 * h + c + 1, :]
            masked = jnp.where(allowed, scores, NEG_FILL)
            top = jnp.max(masked, axis=0, keepdims=True)
            weights = jnp.where(allowed, jnp.exp(masked - top), 0.0)
            tops.append(top)
            totals.append(jnp.sum(weights, axis=0, keepdims=True))
            n_0[h, :, :, chunk(c)] = dot(vt[...], weights.astype(BF16), 1, 0).reshape(RING, SLAB, LANES)
        s_1[h, 0] = jnp.concatenate(tops + totals, axis=0)
    send_all(
        *(spread(12 + h, h, s_1.at[h]) for h in halves), *(scatter(14 + h, h, n_0.at[h], n_1.at[h]) for h in halves)
    )

    def merge(stats, first, others, c):
        top = stats[0][c:c + 1]
        for tile in stats[1:]:
            top = jnp.maximum(top, tile[c:c + 1])
        scales = [jnp.exp(tile[c:c + 1] - top) for tile in stats]
        total = tree_sum([scale * tile[2 + c:3 + c] for scale, tile in zip(scales, stats)])
        numer = tree_sum(
            [first[:, chunk(c)] * scales[0]] + [others[o, :, chunk(c)] * scales[o] for o in range(1, RING)]
        )
        return top, total, numer

    arrive(get_c)
    compact = jnp.concatenate([c_3[h].reshape(DH, HALF).astype(F32).T for h in halves], axis=0).astype(BF16)
    slot_col = jnp.concatenate(
        [jnp.broadcast_to(slots_ref[:, chunk(c)], (LANES, LANES)).T for c in range(CHUNKS)], axis=0
    )
    for c in range(CHUNKS):
        logits = dot(compact, queries[chunk(c), :], 1, 1) * INV_ROOT
        allowed = slot_col <= qp[c:c + 1, :]
        masked = jnp.where(allowed, logits, NEG_FILL)
        top = jnp.max(masked, axis=0, keepdims=True)
        raw = jnp.where(allowed, jnp.exp(masked - top), 0.0)
        feats[:, chunk(c)] = (raw * (1.0 / jnp.sum(raw, axis=0, keepdims=True))).astype(BF16)
    diagonal = lax.broadcasted_iota(jnp.int32, (LANES, LANES), 0) == lax.broadcasted_iota(jnp.int32, (LANES, LANES), 1)
    for i in range(CHUNKS):
        for j in range(i + 1):
            block = dot(feats[chunk(i), :], feats[chunk(j), :], 1, 1)
            gram[i, j] = block + jnp.where(diagonal, RIDGE, 0.0) if i == j else block

    def merge_first():
        arrive([(12 + h, s_1.at[h]) for h in halves] + [(14 + h, n_1.at[h]) for h in halves])
        for h in halves:
            merged = [merge([s_1[h, o] for o in range(RING)], n_0[h, place[h]], n_1[h], c) for c in (0, 1)]
            s_2[h, 0] = jnp.concatenate([m[0] for m in merged] + [m[1] for m in merged], axis=0)
            for c in (0, 1):
                n_2[h, 0, :, chunk(c)] = merged[c][2]
        send_all(
            *(spread(16 + h, 1 - h, s_2.at[h]) for h in halves), *(spread(18 + h, 1 - h, n_2.at[h]) for h in halves)
        )

    def merge_second():
        for h in halves:
            for c in (0, 1):
                _, total, numer = merge([s_2[h, o] for o in range(RING)], n_2[h, 0], n_2[h], c)
                o_3[h, place[h], :, chunk(c)] = (numer / total).astype(BF16)
        send_all(*(gather(20 + h, h, o_3.at[h], place[h]) for h in halves))

    last = CHUNKS - 1

    def after(c):
        if c == MERGE_AFTER:
            arrive([(16 + h, s_2.at[h]) for h in halves] + [(18 + h, n_2.at[h]) for h in halves])
            merge_second()
        if c < last:
            inverse[c] = exact(unit[...], scaled[...], 1, 0)
            for i in range(c + 1, CHUNKS):
                lower[i, c] = exact(gram[i, c], inverse[c], 1, 0)
                upper[c, i] = exact(inverse[c], gram[i, c], 1, 1)
            for i in range(c + 1, CHUNKS):
                for j in range(c + 1, i + 1):
                    gram[i, j] = gram[i, j] - exact(lower[i, c], gram[j, c], 1, 1)
        if c == last - 1:
            arrive([(20 + h, o_3.at[h]) for h in halves])
            attended = jnp.concatenate([o_3[h].reshape(DH, HALF) for h in halves], axis=1)
            row = lax.broadcasted_iota(jnp.int32, (RING, BLOCK), 0)
            column = lax.broadcasted_iota(jnp.int32, (RING, BLOCK), 1)
            pick = jnp.zeros((RING, BLOCK), F32)
            for i in range(RING):
                pick = jnp.where((row == i) & (column == own_id[i]), 1.0, pick)
            own_out[...] = dot(pick.astype(BF16), attended, 1, 1).astype(BF16)
            part = [dot(feats[chunk(i), :], attended, 1, 1) for i in range(CHUNKS)]
            for i in range(1, CHUNKS):
                part[i] = part[i] - close([(lower[i, j], part[j]) for j in range(i)])
            rest[...] = part[last]
            for i in reversed(range(last)):
                part[i] = jnp.concatenate([close([(inverse[i], part[i])]), -upper[i, last]], axis=1)
                if i + 1 < last:
                    part[i] = part[i] - close([(upper[i, j], part[j]) for j in range(i + 1, last)])
                fitted_ref[chunk(i), :] = part[i][:, :DH]
                share[i] = part[i][:, DH:]
            everything = [(2, qp_1), (7, qp_2)] + [
                (stream + h, buffer.at[h])
                for stream, buffer in [
                    (0, q_1), (3, c_1), (5, q_2), (8, c_2), (10, c_3), (12, s_1), (14, n_1), (16, s_2), (18, n_2), (20, o_3)
                ]
                for h in halves
            ]
            for stream, buffer in everything:
                all_of(stream, buffer).wait_send()
        if c == last:
            solved = close([(unit[...], close([(scaled[...], rest[...])]))])
            fitted_ref[chunk(last), :] = solved
            for i in range(last):
                fitted_ref[chunk(i), :] = fitted_ref[chunk(i), :] + close([(share[i], solved)])

    def eliminate(b, carry):
        unit[...], scaled[...] = factor_spd(gram[b, b], lambda: pl.when(b == 0)(merge_first))
        for c in range(CHUNKS):
            pl.when(b == c)(functools.partial(after, c))
        return carry

    lax.fori_loop(0, CHUNKS, eliminate, 0)


MERGE_AFTER = 1
STREAMS = 22


def compaction(queries, qpos, keys, values, slots):
    vmem = pl.BlockSpec(memory_space=pltpu.VMEM)
    table = pltpu.VMEM((2, RING, SLAB, HALF), BF16)
    wide = pltpu.VMEM((2, RING, SLAB, HALF), F32)
    blocks = pltpu.VMEM((CHUNKS, CHUNKS, LANES, LANES), F32)
    stats = pltpu.VMEM((2, RING, CHUNKS, LANES), F32)
    return pl.pallas_call(
        compaction_kernel,
        out_shape=(
            jax.ShapeDtypeStruct((RING, DH), BF16),
            jax.ShapeDtypeStruct((BLOCK, DH), F32),
        ),
        in_specs=[pl.BlockSpec(memory_space=pltpu.HBM)] * 5,
        out_specs=(vmem,) * 2,
        scratch_shapes=[
            pltpu.SMEM((1, RING), jnp.int32),
            pltpu.VMEM((RING, DH), BF16),
            pltpu.VMEM((BLOCK, DH), BF16),
            pltpu.VMEM((BLOCK, DH), BF16),
            pltpu.VMEM((1, BLOCK), jnp.int32),
            pltpu.VMEM((2, RING, QROWS, DH), F32),
            pltpu.VMEM((2, RING, RING * QROWS, DH), BF16),
            pltpu.VMEM((RING, CHUNKS, LANES), jnp.int32),
            pltpu.VMEM((RING, CHUNKS, LANES), jnp.int32),
            table, table, table, table,
            pltpu.VMEM((DH, BLOCK), BF16),
            wide, wide, stats, wide, stats, table,
            pltpu.VMEM((BLOCK, BLOCK), BF16),
            blocks,
            pltpu.VMEM((CHUNKS, LANES, LANES), F32),
            blocks, blocks,
            pltpu.VMEM((CHUNKS, LANES, LANES), F32),
            pltpu.VMEM((LANES, DH), F32),
            pltpu.VMEM((LANES, LANES), F32),
            pltpu.VMEM((LANES, LANES), F32),
            pltpu.SemaphoreType.DMA((5,)),
            pltpu.SemaphoreType.DMA((STREAMS,)),
            pltpu.SemaphoreType.DMA((STREAMS,)),
        ],
        compiler_params=pltpu.CompilerParams(collective_id=0, has_side_effects=True, vmem_limit_bytes=VMEM_LIMIT),
        name="compaction",
    )(qpos, queries, keys, values, slots)


VMEM_LIMIT = 32 * 1024 * 1024


def emit_kernel(own_ref, fitted_ref, own_out, fitted_out):
    own_out[0] = own_ref[...]
    fitted_out[0] = fitted_ref[...]


def emit(own, fitted):
    vmem = pl.BlockSpec(memory_space=pltpu.VMEM)
    return pl.pallas_call(
        emit_kernel,
        out_shape=(
            jax.ShapeDtypeStruct((1, RING, DH), BF16),
            jax.ShapeDtypeStruct((1, BLOCK, DH), F32),
        ),
        in_specs=[vmem] * 2,
        out_specs=(vmem,) * 2,
        compiler_params=pltpu.CompilerParams(vmem_limit_bytes=VMEM_LIMIT),
        name="emit",
    )(own, fitted)


def shards(ref_queries, query_pos, cache_keys, cache_values, slot_index):
    own, fitted = compaction(*(
        pltpu.with_memory_space_constraint(x, pltpu.HBM)
        for x in (ref_queries[0], query_pos, cache_keys[0], cache_values[0], slot_index)
    ))
    return emit(own, fitted)


def solution(mesh):
    in_specs = (
        P("head", "pos", None),
        P("head", "pos"),
        P("head", "pos", None),
        P("head", "pos", None),
        P("head", None),
    )
    out_specs = (P("head", "pos", None), P("head", None, None))
    return jax.shard_map(shards, mesh=mesh, in_specs=in_specs, out_specs=out_specs, check_vma=False)
```

```python
import functools
import math

import jax
import jax.numpy as jnp
from jax import lax
from jax.experimental import pallas as pl
from jax.experimental.pallas import tpu as pltpu
from jax.sharding import PartitionSpec as P

RIDGE = 1.0
NEG_FILL = -1e30
RING = 8
BLOCK = 512
DH = 128
LANES = 128
CHUNKS = BLOCK // LANES
SLAB = DH // RING
HALF = BLOCK // 2
QROWS = 4
INV_ROOT = 1.0 / math.sqrt(DH)
MESH_ID = pl.DeviceIdType.MESH
F32 = jnp.float32
BF16 = jnp.bfloat16


def dot(a, b, ca, cb, precision=None):
    return lax.dot_general(a, b, (((ca,), (cb,)), ((), ())), precision=precision, preferred_element_type=F32)


def chunk(c):
    return slice(c * LANES, (c + 1) * LANES)


def pieces(x):
    high = x.astype(BF16)
    rest = x - high.astype(F32)
    middle = rest.astype(BF16)
    return high, middle, (rest - middle.astype(F32)).astype(BF16)


def stacked(ca, cb, *pairs):
    return dot(
        jnp.concatenate([a for a, _ in pairs], axis=ca), jnp.concatenate([b for _, b in pairs], axis=cb), ca, cb
    )


def exact(a, b, ca, cb):
    ah, am, al = pieces(a)
    bh, bm, bl = pieces(b)
    small = stacked(ca, cb, (ah, bl), (al, bh))
    return small + stacked(ca, cb, (ah, bm), (am, bm)) + stacked(ca, cb, (ah, bh), (am, bh))


def close(pairs):
    split = [(pieces(a), pieces(b)) for a, b in pairs]
    cross_terms = [term for (ah, am, _), (bh, bm, _) in split for term in ((ah, bm), (am, bh))]
    return stacked(1, 0, *cross_terms) + stacked(1, 0, *[(a[0], b[0]) for a, b in split])


def tree_sum(terms):
    while len(terms) > 1:
        terms = [u + v for u, v in zip(terms[::2], terms[1::2])] + ([terms[-1]] if len(terms) % 2 else [])
    return terms[0]


def factor_spd(a, halfway):
    n = a.shape[0]
    sub = lax.broadcasted_iota(jnp.int32, (8, n), 0)
    lane = lax.broadcasted_iota(jnp.int32, (8, n), 1)

    def along(v, j):
        return jnp.broadcast_to(v[:, j:j + 1], (8, n))

    def down(v, i):
        return jnp.broadcast_to(v[i:i + 1, :], (8, n))

    def kept(v):
        return [jnp.where(lane < n + j, u, 0.0) for j, u in enumerate(v)]

    def invert_pivot(m):
        for t in range(0, 8, 2):
            p00, p10, p11 = down(m[t], t), down(m[t], t + 1), down(m[t + 1], t + 1)
            scale = 1.0 / (p00 * p11 - p10 * p10)
            i00, i11, i10 = p11 * scale, p00 * scale, -(p10 * scale)
            f0 = jnp.where(sub == t, -1.0, jnp.where(sub == t + 1, 0.0, m[t]))
            f1 = jnp.where(sub == t + 1, -1.0, jnp.where(sub == t, 0.0, m[t + 1]))
            pivots = (sub == t) | (sub == t + 1)
            new = []
            for j in range(8):
                if j == t:
                    new.append(-(f0 * i00 + f1 * i10))
                elif j == t + 1:
                    new.append(-(f0 * i10 + f1 * i11))
                else:
                    w0, w1 = down(m[j], t), down(m[j], t + 1)
                    x0, x1 = i00 * w0 + i10 * w1, i10 * w0 + i11 * w1
                    new.append(jnp.where(pivots, 0.0, m[j]) - (f0 * x0 + f1 * x1))
            m = new
        return m

    rows = [a[8 * g:8 * g + 8, :] for g in range(n // 8)]
    middle = n // 16
    unit, scaled, unit_half, scaled_half = [], [], [], []

    def solve_row(g, inverted):
        k = 8 * g
        w = jnp.where((lane >= k) & (lane < k + 8), jnp.where(lane - k == sub, 1.0, 0.0), rows[g])
        x = tree_sum([inverted[j] * down(w, j) for j in range(8)])
        unit.append(jnp.where(lane < k + 8, w, 0.0))
        scaled.append(jnp.where(lane < k + 8, x, 0.0))
        if g < middle:
            unit_half.append(w)
            scaled_half.append(jnp.where((lane < k + 8) | (lane >= n // 2), x, 0.0))
        return [down(x, j) for j in range(8)]

    def eliminate_row(g, of, factors, xs):
        k = 8 * of
        own = (lane >= k) & (lane < k + 8)
        rows[g] = jnp.where(own, 0.0, rows[g]) - tree_sum([factors[j] * xs[j] for j in range(8)])

    for g0 in range(0, n // 8, 2):
        if g0 == middle:
            halfway()
            share = exact(jnp.concatenate(unit_half, axis=0).T[n // 2:, :], jnp.concatenate(scaled_half, axis=0), 1, 0)
            for g in range(middle, n // 8):
                rows[g] = jnp.where(lane < n // 2, 0.0, rows[g]) - share[8 * (g - middle):8 * (g - middle) + 8, :]
        g1 = g0 + 1
        m = kept([along(rows[g0], 8 * g0 + j) for j in range(8)])
        b = kept([along(rows[g1], 8 * g0 + j) for j in range(8)])
        m1 = [along(rows[g1], 8 * g1 + j) for j in range(8)]
        later = range(g0 + 2, middle if g0 < middle else n // 8)
        factors = {g: [along(rows[g], 8 * g0 + j) for j in range(8)] for g in later}
        m = invert_pivot(m)
        bm = [tree_sum([b[i] * down(m[j], i) for i in range(8)]) for j in range(8)]
        m1 = [m1[j] - tree_sum([bm[i] * down(b[i], j) for i in range(8)]) for j in range(8)]
        xs = solve_row(g0, m)
        eliminate_row(g1, g0, b, xs)
        for g in later:
            eliminate_row(g, g0, factors[g], xs)
        factors = {g: [along(rows[g], 8 * g1 + j) for j in range(8)] for g in later}
        m1 = invert_pivot(m1)
        xs = solve_row(g1, m1)
        for g in later:
            eliminate_row(g, g1, factors[g], xs)
    return jnp.concatenate(unit, axis=0).T, jnp.concatenate(scaled, axis=0)


def compaction_kernel(
    qpos_hbm, q_hbm, k_hbm, v_hbm, slots_hbm,
    own_out, fitted_ref,
    qpos_ref, q_ref, k_ref, v_ref, slots_ref,
    q_1, q_2, qp_1, qp_2, c_0, c_1, c_2, c_3, vt, n_0, n_1, s_1, n_2, s_2, o_3, feats, gram, inverse, lower, upper, share, rest, unit, scaled, slot_col,
    load_sems, send_sems, recv_sems,
):
    me = lax.axis_index("pos")
    place = (lax.div(me, RING), lax.rem(me, RING))

    def peer(axis, o):
        if axis == 0:
            return {"pos": lax.rem(place[0] + o, RING) * RING + place[1]}
        return {"pos": place[0] * RING + lax.rem(place[1] + o, RING)}

    offsets = (4, 3, 5, 2, 6, 1, 7)
    barrier = pltpu.get_barrier_semaphore()
    for o in offsets:
        for axis in (0, 1):
            pl.semaphore_signal(barrier, inc=1, device_id=peer(axis, o), device_id_type=MESH_ID)

    loads = [
        pltpu.make_async_copy(src, dst, load_sems.at[i])
        for i, (src, dst) in enumerate([
            (slots_hbm, slots_ref), (k_hbm, k_ref), (qpos_hbm, qpos_ref), (q_hbm, q_ref), (v_hbm, v_ref),
        ])
    ]
    for load in loads:
        load.start()
    for load in loads[:4]:
        load.wait()

    def copy_of(stream, axis, o, src, dst):
        return pltpu.make_async_remote_copy(
            src_ref=src, dst_ref=dst, send_sem=send_sems.at[stream], recv_sem=recv_sems.at[stream],
            device_id=peer(axis, o), device_id_type=MESH_ID,
        )

    def all_of(stream, buffer):
        seven = buffer.at[pl.ds(0, RING - 1)]
        return copy_of(stream, 0, 1, seven, seven)

    def send_all(*streams):
        for o in offsets:
            for stream, axis, src_of, dst_of, _ in streams:
                copy_of(stream, axis, o, src_of(o), dst_of(o)).start()
        return [(stream, buffer) for stream, _, _, _, buffer in streams]

    def gather(stream, axis, buffer, slot):
        return (stream, axis, lambda o: buffer.at[slot], lambda o: buffer.at[slot], buffer)

    def spread(stream, axis, buffer):
        return (stream, axis, lambda o: buffer.at[0], lambda o: buffer.at[o], buffer)

    def scatter(stream, axis, source, buffer):
        return (
            stream, axis, lambda o: source.at[lax.rem(place[axis] + o, RING)], lambda o: buffer.at[o], buffer
        )

    def arrive(streams):
        for stream, buffer in streams:
            all_of(stream, buffer).wait_recv()

    def sent(tables):
        for stream, buffer in tables:
            for h in (0, 1):
                all_of(stream + h, buffer.at[h]).wait_send()

    halves = (0, 1)

    base = me * BLOCK
    lane_id = (
        lax.broadcasted_iota(jnp.int32, (CHUNKS, LANES), 0) * LANES
        + lax.broadcasted_iota(jnp.int32, (CHUNKS, LANES), 1)
    )
    own_id = [
        HALF * h + place[h] * (RING * QROWS) + place[1 - h] * QROWS + i for h in halves for i in range(QROWS)
    ]
    tile = jnp.zeros((CHUNKS, LANES), jnp.int32)
    for i in range(RING):
        tile = jnp.where(lane_id == own_id[i], qpos_ref[0, i], tile)
    qp_1[0] = tile
    own_q = q_ref[...].astype(F32)
    for h in halves:
        q_1[h, place[1 - h]] = own_q[QROWS * h:QROWS * h + QROWS, :]
    position = lax.broadcasted_iota(jnp.int32, (BLOCK, BLOCK), 0) + base
    one_hot = jnp.where(position == slots_ref[...], 1.0, 0.0).astype(BF16)
    picked = dot(k_ref[...], one_hot, 0, 0).astype(BF16)
    for h in halves:
        c_0[h] = picked[:, h * HALF:(h + 1) * HALF].reshape(RING, SLAB, HALF)

    pl.semaphore_wait(barrier, 2 * (RING - 1))

    get_q = send_all(*(gather(h, 1 - h, q_1.at[h], place[1 - h]) for h in halves))
    get_qp = send_all(spread(2, 1, qp_1))
    get_c = send_all(*(scatter(3 + h, h, c_0.at[h], c_1.at[h]) for h in halves))
    loads[4].wait()
    vt[...] = v_ref[...].astype(F32).T.astype(BF16)

    arrive(get_q)
    for h in halves:
        q_2[h, place[h]] = q_1[h].reshape(RING * QROWS, DH).astype(BF16)
    get_q = send_all(*(gather(5 + h, h, q_2.at[h], place[h]) for h in halves))
    arrive(get_qp)
    qp_2[0] = tree_sum([qp_1[o] for o in range(RING)])
    get_qp = send_all(spread(7, 0, qp_2))

    arrive(get_c)
    for h in halves:
        c_2[h, 0] = tree_sum([c_0[h, place[h]].astype(F32)] + [c_1[h, o].astype(F32) for o in offsets]).astype(BF16)
    get_c = send_all(*(spread(8 + h, 1 - h, c_2.at[h]) for h in halves))

    arrive(get_q)
    arrive(get_qp)
    qp = tree_sum([qp_2[o] for o in range(RING)])
    queries = q_2[...].reshape(BLOCK, DH)

    arrive(get_c)
    for h in halves:
        c_3[h, place[h]] = tree_sum([c_2[h, o].astype(F32) for o in range(RING)]).astype(BF16)
    get_c = send_all(*(gather(10 + h, h, c_3.at[h], place[h]) for h in halves))

    key_pos = lax.broadcasted_iota(jnp.int32, (BLOCK, LANES), 0) + base
    for h in halves:
        tops, totals = [], []
        for c in (0, 1):
            scores = dot(k_ref[...], queries[chunk(2 * h + c), :], 1, 1) * INV_ROOT
            allowed = key_pos <= qp[2 * h + c:2 * h + c + 1, :]
            masked = jnp.where(allowed, scores, NEG_FILL)
            top = jnp.max(masked, axis=0, keepdims=True)
            weights = jnp.where(allowed, jnp.exp(masked - top), 0.0)
            tops.append(top)
            totals.append(jnp.sum(weights, axis=0, keepdims=True))
            n_0[h, :, :, chunk(c)] = dot(vt[...], weights.astype(BF16), 1, 0).reshape(RING, SLAB, LANES)
        s_1[h, 0] = jnp.concatenate(tops + totals, axis=0)
    send_all(
        *(spread(12 + h, h, s_1.at[h]) for h in halves), *(scatter(14 + h, h, n_0.at[h], n_1.at[h]) for h in halves)
    )

    def merge(stats, first, others, c):
        top = stats[0][c:c + 1]
        for tile in stats[1:]:
            top = jnp.maximum(top, tile[c:c + 1])
        scales = [jnp.exp(tile[c:c + 1] - top) for tile in stats]
        total = tree_sum([scale * tile[2 + c:3 + c] for scale, tile in zip(scales, stats)])
        numer = tree_sum(
            [first[:, chunk(c)] * scales[0]] + [others[o, :, chunk(c)] * scales[o] for o in range(1, RING)]
        )
        return top, total, numer

    for c in range(CHUNKS):
        slot_col[chunk(c), :] = jnp.broadcast_to(slots_ref[:, chunk(c)], (LANES, LANES)).T
    all_of(2, qp_1).wait_send()
    all_of(7, qp_2).wait_send()
    sent([(0, q_1), (3, c_1), (5, q_2), (8, c_2)])
    arrive(get_c)
    compact = jnp.concatenate([c_3[h].reshape(DH, HALF).astype(F32).T for h in halves], axis=0).astype(BF16)
    for c in range(CHUNKS):
        logits = dot(compact, queries[chunk(c), :], 1, 1) * INV_ROOT
        allowed = slot_col[...] <= qp[c:c + 1, :]
        masked = jnp.where(allowed, logits, NEG_FILL)
        top = jnp.max(masked, axis=0, keepdims=True)
        raw = jnp.where(allowed, jnp.exp(masked - top), 0.0)
        feats[:, chunk(c)] = (raw * (1.0 / jnp.sum(raw, axis=0, keepdims=True))).astype(BF16)
    diagonal = lax.broadcasted_iota(jnp.int32, (LANES, LANES), 0) == lax.broadcasted_iota(jnp.int32, (LANES, LANES), 1)
    for i in range(CHUNKS):
        for j in range(i + 1):
            block = dot(feats[chunk(i), :], feats[chunk(j), :], 1, 1)
            gram[i, j] = block + jnp.where(diagonal, RIDGE, 0.0) if i == j else block

    def merge_first():
        arrive([(12 + h, s_1.at[h]) for h in halves] + [(14 + h, n_1.at[h]) for h in halves])
        for h in halves:
            merged = [merge([s_1[h, o] for o in range(RING)], n_0[h, place[h]], n_1[h], c) for c in (0, 1)]
            s_2[h, 0] = jnp.concatenate([m[0] for m in merged] + [m[1] for m in merged], axis=0)
            for c in (0, 1):
                n_2[h, 0, :, chunk(c)] = merged[c][2]
        send_all(
            *(spread(16 + h, 1 - h, s_2.at[h]) for h in halves), *(spread(18 + h, 1 - h, n_2.at[h]) for h in halves)
        )

    def merge_second():
        for h in halves:
            for c in (0, 1):
                _, total, numer = merge([s_2[h, o] for o in range(RING)], n_2[h, 0], n_2[h], c)
                o_3[h, place[h], :, chunk(c)] = (numer / total).astype(BF16)
        send_all(*(gather(20 + h, h, o_3.at[h], place[h]) for h in halves))

    last = CHUNKS - 1

    def after(c):
        if c == MERGE_AFTER:
            arrive([(16 + h, s_2.at[h]) for h in halves] + [(18 + h, n_2.at[h]) for h in halves])
            merge_second()
        if c < last:
            inverse[c] = exact(unit[...], scaled[...], 1, 0)
            for i in range(c + 1, CHUNKS):
                lower[i, c] = exact(gram[i, c], inverse[c], 1, 0)
                upper[c, i] = lower[i, c].T
            for i in range(c + 1, CHUNKS):
                for j in range(c + 1, i + 1):
                    gram[i, j] = gram[i, j] - exact(lower[i, c], gram[j, c], 1, 1)
        if c == last - 1:
            sent([(10, c_3), (12, s_1), (14, n_1), (16, s_2), (18, n_2)])
            arrive([(20 + h, o_3.at[h]) for h in halves])
            attended = jnp.concatenate([o_3[h].reshape(DH, HALF) for h in halves], axis=1)
            row = lax.broadcasted_iota(jnp.int32, (RING, BLOCK), 0)
            column = lax.broadcasted_iota(jnp.int32, (RING, BLOCK), 1)
            pick = jnp.zeros((RING, BLOCK), F32)
            for i in range(RING):
                pick = jnp.where((row == i) & (column == own_id[i]), 1.0, pick)
            own_out[...] = dot(pick.astype(BF16), attended, 1, 1).astype(BF16)
            part = [dot(feats[chunk(i), :], attended, 1, 1) for i in range(CHUNKS)]
            for i in range(1, CHUNKS):
                part[i] = part[i] - close([(lower[i, j], part[j]) for j in range(i)])
            rest[...] = part[last]
            for i in reversed(range(last)):
                part[i] = jnp.concatenate([close([(inverse[i], part[i])]), -upper[i, last]], axis=1)
                if i + 1 < last:
                    part[i] = part[i] - close([(upper[i, j], part[j]) for j in range(i + 1, last)])
                fitted_ref[chunk(i), :] = part[i][:, :DH]
                share[i] = part[i][:, DH:]
            sent([(20, o_3)])
        if c == last:
            solved = close([(unit[...], close([(scaled[...], rest[...])]))])
            fitted_ref[chunk(last), :] = solved
            for i in range(last):
                fitted_ref[chunk(i), :] = fitted_ref[chunk(i), :] + close([(share[i], solved)])

    def eliminate(b, carry):
        unit[...], scaled[...] = factor_spd(gram[b, b], lambda: pl.when(b == 0)(merge_first))
        for c in range(CHUNKS):
            pl.when(b == c)(functools.partial(after, c))
        return carry

    lax.fori_loop(0, CHUNKS, eliminate, 0)


MERGE_AFTER = 1
STREAMS = 22


def compaction(queries, qpos, keys, values, slots):
    vmem = pl.BlockSpec(memory_space=pltpu.VMEM)
    table = pltpu.VMEM((2, RING, SLAB, HALF), BF16)
    wide = pltpu.VMEM((2, RING, SLAB, HALF), F32)
    blocks = pltpu.VMEM((CHUNKS, CHUNKS, LANES, LANES), F32)
    stats = pltpu.VMEM((2, RING, CHUNKS, LANES), F32)
    return pl.pallas_call(
        compaction_kernel,
        out_shape=(
            jax.ShapeDtypeStruct((RING, DH), BF16),
            jax.ShapeDtypeStruct((BLOCK, DH), F32),
        ),
        in_specs=[pl.BlockSpec(memory_space=pltpu.HBM)] * 5,
        out_specs=(vmem,) * 2,
        scratch_shapes=[
            pltpu.SMEM((1, RING), jnp.int32),
            pltpu.VMEM((RING, DH), BF16),
            pltpu.VMEM((BLOCK, DH), BF16),
            pltpu.VMEM((BLOCK, DH), BF16),
            pltpu.VMEM((1, BLOCK), jnp.int32),
            pltpu.VMEM((2, RING, QROWS, DH), F32),
            pltpu.VMEM((2, RING, RING * QROWS, DH), BF16),
            pltpu.VMEM((RING, CHUNKS, LANES), jnp.int32),
            pltpu.VMEM((RING, CHUNKS, LANES), jnp.int32),
            table, table, table, table,
            pltpu.VMEM((DH, BLOCK), BF16),
            wide, wide, stats, wide, stats, table,
            pltpu.VMEM((BLOCK, BLOCK), BF16),
            blocks,
            pltpu.VMEM((CHUNKS, LANES, LANES), F32),
            blocks, blocks,
            pltpu.VMEM((CHUNKS, LANES, LANES), F32),
            pltpu.VMEM((LANES, DH), F32),
            pltpu.VMEM((LANES, LANES), F32),
            pltpu.VMEM((LANES, LANES), F32),
            pltpu.VMEM((BLOCK, LANES), jnp.int32),
            pltpu.SemaphoreType.DMA((5,)),
            pltpu.SemaphoreType.DMA((STREAMS,)),
            pltpu.SemaphoreType.DMA((STREAMS,)),
        ],
        compiler_params=pltpu.CompilerParams(collective_id=0, has_side_effects=True, vmem_limit_bytes=VMEM_LIMIT),
        name="compaction",
    )(qpos, queries, keys, values, slots)


VMEM_LIMIT = 32 * 1024 * 1024


def emit_kernel(own_ref, fitted_ref, own_out, fitted_out):
    own_out[0] = own_ref[...]
    fitted_out[0] = fitted_ref[...]


def emit(own, fitted):
    vmem = pl.BlockSpec(memory_space=pltpu.VMEM)
    return pl.pallas_call(
        emit_kernel,
        out_shape=(
            jax.ShapeDtypeStruct((1, RING, DH), BF16),
            jax.ShapeDtypeStruct((1, BLOCK, DH), F32),
        ),
        in_specs=[vmem] * 2,
        out_specs=(vmem,) * 2,
        compiler_params=pltpu.CompilerParams(vmem_limit_bytes=VMEM_LIMIT),
        name="emit",
    )(own, fitted)


def shards(ref_queries, query_pos, cache_keys, cache_values, slot_index):
    own, fitted = compaction(*(
        pltpu.with_memory_space_constraint(x, pltpu.HBM)
        for x in (ref_queries[0], query_pos, cache_keys[0], cache_values[0], slot_index)
    ))
    return emit(own, fitted)


def solution(mesh):
    in_specs = (
        P("head", "pos", None),
        P("head", "pos"),
        P("head", "pos", None),
        P("head", "pos", None),
        P("head", None),
    )
    out_specs = (P("head", "pos", None), P("head", None, None))
    return jax.shard_map(shards, mesh=mesh, in_specs=in_specs, out_specs=out_specs, check_vma=False)
```

```python
import functools
import math

import jax
import jax.numpy as jnp
from jax import lax
from jax.experimental import pallas as pl
from jax.experimental.pallas import tpu as pltpu
from jax.sharding import PartitionSpec as P

RIDGE = 1.0
NEG_FILL = -1e30
RING = 8
BLOCK = 512
DH = 128
LANES = 128
CHUNKS = BLOCK // LANES
SLAB = DH // RING
HALF = BLOCK // 2
QROWS = 4
INV_ROOT = 1.0 / math.sqrt(DH)
MESH_ID = pl.DeviceIdType.MESH
F32 = jnp.float32
BF16 = jnp.bfloat16


def dot(a, b, ca, cb, precision=None):
    return lax.dot_general(a, b, (((ca,), (cb,)), ((), ())), precision=precision, preferred_element_type=F32)


def chunk(c):
    return slice(c * LANES, (c + 1) * LANES)


def pieces(x):
    high = x.astype(BF16)
    rest = x - high.astype(F32)
    middle = rest.astype(BF16)
    return high, middle, (rest - middle.astype(F32)).astype(BF16)


def stacked(ca, cb, *pairs):
    return dot(
        jnp.concatenate([a for a, _ in pairs], axis=ca), jnp.concatenate([b for _, b in pairs], axis=cb), ca, cb
    )


def exact(a, b, ca, cb):
    ah, am, al = pieces(a)
    bh, bm, bl = pieces(b)
    small = stacked(ca, cb, (ah, bl), (al, bh))
    return small + stacked(ca, cb, (ah, bm), (am, bm)) + stacked(ca, cb, (ah, bh), (am, bh))


def close(pairs):
    split = [(pieces(a), pieces(b)) for a, b in pairs]
    cross_terms = [term for (ah, am, _), (bh, bm, _) in split for term in ((ah, bm), (am, bh))]
    return stacked(1, 0, *cross_terms) + stacked(1, 0, *[(a[0], b[0]) for a, b in split])


def tree_sum(terms):
    while len(terms) > 1:
        terms = [u + v for u, v in zip(terms[::2], terms[1::2])] + ([terms[-1]] if len(terms) % 2 else [])
    return terms[0]


def factor_spd(a, halfway):
    n = a.shape[0]
    sub = lax.broadcasted_iota(jnp.int32, (8, n), 0)
    lane = lax.broadcasted_iota(jnp.int32, (8, n), 1)

    def along(v, j):
        return jnp.broadcast_to(v[:, j:j + 1], (8, n))

    def down(v, i):
        return jnp.broadcast_to(v[i:i + 1, :], (8, n))

    def kept(v):
        return [jnp.where(lane < n + j, u, 0.0) for j, u in enumerate(v)]

    def invert_pivot(m):
        for t in range(0, 8, 2):
            p00, p10, p11 = down(m[t], t), down(m[t], t + 1), down(m[t + 1], t + 1)
            scale = 1.0 / (p00 * p11 - p10 * p10)
            i00, i11, i10 = p11 * scale, p00 * scale, -(p10 * scale)
            f0 = jnp.where(sub == t, -1.0, jnp.where(sub == t + 1, 0.0, m[t]))
            f1 = jnp.where(sub == t + 1, -1.0, jnp.where(sub == t, 0.0, m[t + 1]))
            pivots = (sub == t) | (sub == t + 1)
            new = []
            for j in range(8):
                if j == t:
                    new.append(-(f0 * i00 + f1 * i10))
                elif j == t + 1:
                    new.append(-(f0 * i10 + f1 * i11))
                else:
                    w0, w1 = down(m[j], t), down(m[j], t + 1)
                    x0, x1 = i00 * w0 + i10 * w1, i10 * w0 + i11 * w1
                    new.append(jnp.where(pivots, 0.0, m[j]) - (f0 * x0 + f1 * x1))
            m = new
        return m

    rows = [a[8 * g:8 * g + 8, :] for g in range(n // 8)]
    middle = n // 16
    unit, scaled, unit_half, scaled_half = [], [], [], []

    def solve_row(g, inverted):
        k = 8 * g
        w = jnp.where((lane >= k) & (lane < k + 8), jnp.where(lane - k == sub, 1.0, 0.0), rows[g])
        x = tree_sum([inverted[j] * down(w, j) for j in range(8)])
        unit.append(jnp.where(lane < k + 8, w, 0.0))
        scaled.append(jnp.where(lane < k + 8, x, 0.0))
        if g < middle:
            unit_half.append(w)
            scaled_half.append(jnp.where((lane < k + 8) | (lane >= n // 2), x, 0.0))
        return [down(x, j) for j in range(8)]

    def eliminate_row(g, of, factors, xs):
        k = 8 * of
        own = (lane >= k) & (lane < k + 8)
        rows[g] = jnp.where(own, 0.0, rows[g]) - tree_sum([factors[j] * xs[j] for j in range(8)])

    for g0 in range(0, n // 8, 2):
        if g0 == middle:
            halfway()
            share = exact(jnp.concatenate(unit_half, axis=0).T[n // 2:, :], jnp.concatenate(scaled_half, axis=0), 1, 0)
            for g in range(middle, n // 8):
                rows[g] = jnp.where(lane < n // 2, 0.0, rows[g]) - share[8 * (g - middle):8 * (g - middle) + 8, :]
        g1 = g0 + 1
        m = kept([along(rows[g0], 8 * g0 + j) for j in range(8)])
        b = kept([along(rows[g1], 8 * g0 + j) for j in range(8)])
        m1 = [along(rows[g1], 8 * g1 + j) for j in range(8)]
        later = range(g0 + 2, middle if g0 < middle else n // 8)
        factors = {g: [along(rows[g], 8 * g0 + j) for j in range(8)] for g in later}
        m = invert_pivot(m)
        bm = [tree_sum([b[i] * down(m[j], i) for i in range(8)]) for j in range(8)]
        m1 = [m1[j] - tree_sum([bm[i] * down(b[i], j) for i in range(8)]) for j in range(8)]
        xs = solve_row(g0, m)
        eliminate_row(g1, g0, b, xs)
        for g in later:
            eliminate_row(g, g0, factors[g], xs)
        factors = {g: [along(rows[g], 8 * g1 + j) for j in range(8)] for g in later}
        m1 = invert_pivot(m1)
        xs = solve_row(g1, m1)
        for g in later:
            eliminate_row(g, g1, factors[g], xs)
    return jnp.concatenate(unit, axis=0).T, jnp.concatenate(scaled, axis=0)


def compaction_kernel(
    qpos_hbm, q_hbm, k_hbm, v_hbm, slots_hbm,
    own_out, fitted_ref,
    qpos_ref, q_ref, k_ref, v_ref, slots_ref,
    q_1, q_2, qp_1, qp_2, c_0, c_1, c_2, c_3, vt, n_0, n_1, s_1, n_2, s_2, o_3, feats, gram, inverse, lower, upper, share, rest, unit, scaled, slot_col,
    load_sems, send_sems, recv_sems,
):
    me = lax.axis_index("pos")
    place = (lax.div(me, RING), lax.rem(me, RING))

    def peer(axis, o):
        if axis == 0:
            return {"pos": lax.rem(place[0] + o, RING) * RING + place[1]}
        return {"pos": place[0] * RING + lax.rem(place[1] + o, RING)}

    offsets = (4, 3, 5, 2, 6, 1, 7)
    barrier = pltpu.get_barrier_semaphore()
    for o in offsets:
        for axis in (0, 1):
            pl.semaphore_signal(barrier, inc=1, device_id=peer(axis, o), device_id_type=MESH_ID)

    loads = [
        pltpu.make_async_copy(src, dst, load_sems.at[i])
        for i, (src, dst) in enumerate([
            (slots_hbm, slots_ref), (k_hbm, k_ref), (qpos_hbm, qpos_ref), (q_hbm, q_ref), (v_hbm, v_ref),
        ])
    ]
    for load in loads:
        load.start()
    for load in loads[:4]:
        load.wait()

    def copy_of(stream, axis, o, src, dst):
        return pltpu.make_async_remote_copy(
            src_ref=src, dst_ref=dst, send_sem=send_sems.at[stream], recv_sem=recv_sems.at[stream],
            device_id=peer(axis, o), device_id_type=MESH_ID,
        )

    def all_of(stream, buffer):
        seven = buffer.at[pl.ds(0, RING - 1)]
        return copy_of(stream, 0, 1, seven, seven)

    def send_all(*streams):
        for o in offsets:
            for stream, axis, src_of, dst_of, _ in streams:
                copy_of(stream, axis, o, src_of(o), dst_of(o)).start()
        return [(stream, buffer) for stream, _, _, _, buffer in streams]

    def gather(stream, axis, buffer, slot):
        return (stream, axis, lambda o: buffer.at[slot], lambda o: buffer.at[slot], buffer)

    def spread(stream, axis, buffer):
        return (stream, axis, lambda o: buffer.at[0], lambda o: buffer.at[o], buffer)

    def scatter(stream, axis, source, buffer):
        return (
            stream, axis, lambda o: source.at[lax.rem(place[axis] + o, RING)], lambda o: buffer.at[o], buffer
        )

    def arrive(streams):
        for stream, buffer in streams:
            all_of(stream, buffer).wait_recv()

    def sent(tables):
        for stream, buffer in tables:
            for h in (0, 1):
                all_of(stream + h, buffer.at[h]).wait_send()

    halves = (0, 1)

    base = me * BLOCK
    lane_id = (
        lax.broadcasted_iota(jnp.int32, (CHUNKS, LANES), 0) * LANES
        + lax.broadcasted_iota(jnp.int32, (CHUNKS, LANES), 1)
    )
    own_id = [
        HALF * h + place[h] * (RING * QROWS) + place[1 - h] * QROWS + i for h in halves for i in range(QROWS)
    ]
    tile = jnp.zeros((CHUNKS, LANES), jnp.int32)
    for i in range(RING):
        tile = jnp.where(lane_id == own_id[i], qpos_ref[0, i], tile)
    qp_1[0] = tile
    own_q = q_ref[...].astype(F32)
    for h in halves:
        q_1[h, place[1 - h]] = own_q[QROWS * h:QROWS * h + QROWS, :]
    position = lax.broadcasted_iota(jnp.int32, (BLOCK, BLOCK), 0) + base
    one_hot = jnp.where(position == slots_ref[...], 1.0, 0.0).astype(BF16)
    picked = dot(k_ref[...], one_hot, 0, 0).astype(BF16)
    for h in halves:
        c_0[h] = picked[:, h * HALF:(h + 1) * HALF].reshape(RING, SLAB, HALF)

    pl.semaphore_wait(barrier, 2 * (RING - 1))

    get_q = send_all(*(gather(h, 1 - h, q_1.at[h], place[1 - h]) for h in halves))
    get_qp = send_all(spread(2, 1, qp_1))
    get_c = send_all(*(scatter(3 + h, h, c_0.at[h], c_1.at[h]) for h in halves))
    loads[4].wait()
    vt[...] = v_ref[...].astype(F32).T.astype(BF16)

    arrive(get_q)
    for h in halves:
        q_2[h, place[h]] = q_1[h].reshape(RING * QROWS, DH).astype(BF16)
    get_q = send_all(*(gather(5 + h, h, q_2.at[h], place[h]) for h in halves))
    arrive(get_qp)
    qp_2[0] = tree_sum([qp_1[o] for o in range(RING)])
    get_qp = send_all(spread(7, 0, qp_2))

    arrive(get_c)
    for h in halves:
        c_2[h, 0] = tree_sum([c_0[h, place[h]].astype(F32)] + [c_1[h, o].astype(F32) for o in offsets]).astype(BF16)
    get_c = send_all(*(spread(8 + h, 1 - h, c_2.at[h]) for h in halves))

    arrive(get_q)
    arrive(get_qp)
    qp = tree_sum([qp_2[o] for o in range(RING)])
    queries = q_2[...].reshape(BLOCK, DH)

    arrive(get_c)
    for h in halves:
        c_3[h, place[h]] = tree_sum([c_2[h, o].astype(F32) for o in range(RING)]).astype(BF16)
    get_c = send_all(*(gather(10 + h, h, c_3.at[h], place[h]) for h in halves))

    key_pos = lax.broadcasted_iota(jnp.int32, (BLOCK, LANES), 0) + base
    for h in halves:
        tops, totals = [], []
        for c in (0, 1):
            scores = dot(k_ref[...], queries[chunk(2 * h + c), :], 1, 1) * INV_ROOT
            allowed = key_pos <= qp[2 * h + c:2 * h + c + 1, :]
            masked = jnp.where(allowed, scores, NEG_FILL)
            top = jnp.max(masked, axis=0, keepdims=True)
            weights = jnp.where(allowed, jnp.exp(masked - top), 0.0)
            tops.append(top)
            totals.append(jnp.sum(weights, axis=0, keepdims=True))
            n_0[h, :, :, chunk(c)] = dot(vt[...], weights.astype(BF16), 1, 0).reshape(RING, SLAB, LANES)
        s_1[h, 0] = jnp.concatenate(tops + totals, axis=0)
    send_all(
        *(spread(12 + h, h, s_1.at[h]) for h in halves), *(scatter(14 + h, h, n_0.at[h], n_1.at[h]) for h in halves)
    )

    def merge(stats, first, others, c):
        top = stats[0][c:c + 1]
        for tile in stats[1:]:
            top = jnp.maximum(top, tile[c:c + 1])
        scales = [jnp.exp(tile[c:c + 1] - top) for tile in stats]
        total = tree_sum([scale * tile[2 + c:3 + c] for scale, tile in zip(scales, stats)])
        numer = tree_sum(
            [first[:, chunk(c)] * scales[0]] + [others[o, :, chunk(c)] * scales[o] for o in range(1, RING)]
        )
        return top, total, numer

    for c in range(CHUNKS):
        slot_col[chunk(c), :] = jnp.broadcast_to(slots_ref[:, chunk(c)], (LANES, LANES)).T
    all_of(2, qp_1).wait_send()
    all_of(7, qp_2).wait_send()
    sent([(0, q_1), (3, c_1), (5, q_2), (8, c_2)])
    arrive(get_c)
    compact = jnp.concatenate([c_3[h].reshape(DH, HALF).astype(F32).T for h in halves], axis=0).astype(BF16)
    for c in range(CHUNKS):
        logits = dot(compact, queries[chunk(c), :], 1, 1) * INV_ROOT
        allowed = slot_col[...] <= qp[c:c + 1, :]
        masked = jnp.where(allowed, logits, NEG_FILL)
        top = jnp.max(masked, axis=0, keepdims=True)
        raw = jnp.where(allowed, jnp.exp(masked - top), 0.0)
        feats[:, chunk(c)] = (raw * (1.0 / jnp.sum(raw, axis=0, keepdims=True))).astype(BF16)
    diagonal = lax.broadcasted_iota(jnp.int32, (LANES, LANES), 0) == lax.broadcasted_iota(jnp.int32, (LANES, LANES), 1)
    for i in range(CHUNKS):
        for j in range(i + 1):
            block = dot(feats[chunk(i), :], feats[chunk(j), :], 1, 1)
            gram[i, j] = block + jnp.where(diagonal, RIDGE, 0.0) if i == j else block

    def merge_first():
        arrive([(12 + h, s_1.at[h]) for h in halves] + [(14 + h, n_1.at[h]) for h in halves])
        for h in halves:
            merged = [merge([s_1[h, o] for o in range(RING)], n_0[h, place[h]], n_1[h], c) for c in (0, 1)]
            s_2[h, 0] = jnp.concatenate([m[0] for m in merged] + [m[1] for m in merged], axis=0)
            for c in (0, 1):
                n_2[h, 0, :, chunk(c)] = merged[c][2]
        send_all(
            *(spread(16 + h, 1 - h, s_2.at[h]) for h in halves), *(spread(18 + h, 1 - h, n_2.at[h]) for h in halves)
        )

    def merge_second():
        arrive([(16 + h, s_2.at[h]) for h in halves] + [(18 + h, n_2.at[h]) for h in halves])
        for h in halves:
            for c in (0, 1):
                _, total, numer = merge([s_2[h, o] for o in range(RING)], n_2[h, 0], n_2[h], c)
                o_3[h, place[h], :, chunk(c)] = (numer / total).astype(BF16)
        send_all(*(gather(20 + h, h, o_3.at[h], place[h]) for h in halves))

    last = CHUNKS - 1

    def after(c):
        if c < last:
            inverse[c] = exact(unit[...], scaled[...], 1, 0)
            for i in range(c + 1, CHUNKS):
                lower[i, c] = exact(gram[i, c], inverse[c], 1, 0)
                upper[c, i] = lower[i, c].T
            for i in range(c + 1, CHUNKS):
                for j in range(c + 1, i + 1):
                    gram[i, j] = gram[i, j] - exact(lower[i, c], gram[j, c], 1, 1)
        if c == last - 1:
            sent([(10, c_3), (12, s_1), (14, n_1), (16, s_2), (18, n_2)])
            arrive([(20 + h, o_3.at[h]) for h in halves])
            attended = jnp.concatenate([o_3[h].reshape(DH, HALF) for h in halves], axis=1)
            row = lax.broadcasted_iota(jnp.int32, (RING, BLOCK), 0)
            column = lax.broadcasted_iota(jnp.int32, (RING, BLOCK), 1)
            pick = jnp.zeros((RING, BLOCK), F32)
            for i in range(RING):
                pick = jnp.where((row == i) & (column == own_id[i]), 1.0, pick)
            own_out[...] = dot(pick.astype(BF16), attended, 1, 1).astype(BF16)
            part = [dot(feats[chunk(i), :], attended, 1, 1) for i in range(CHUNKS)]
            for i in range(1, CHUNKS):
                part[i] = part[i] - close([(lower[i, j], part[j]) for j in range(i)])
            rest[...] = part[last]
            for i in reversed(range(last)):
                part[i] = jnp.concatenate([close([(inverse[i], part[i])]), -upper[i, last]], axis=1)
                if i + 1 < last:
                    part[i] = part[i] - close([(upper[i, j], part[j]) for j in range(i + 1, last)])
                fitted_ref[chunk(i), :] = part[i][:, :DH]
                share[i] = part[i][:, DH:]
            sent([(20, o_3)])
        if c == last:
            solved = close([(unit[...], close([(scaled[...], rest[...])]))])
            fitted_ref[chunk(last), :] = solved
            for i in range(last):
                fitted_ref[chunk(i), :] = fitted_ref[chunk(i), :] + close([(share[i], solved)])

    def eliminate(b, carry):
        def halfway():
            pl.when(b == 0)(merge_first)
            pl.when(b == 1)(merge_second)

        unit[...], scaled[...] = factor_spd(gram[b, b], halfway)
        for c in range(CHUNKS):
            pl.when(b == c)(functools.partial(after, c))
        return carry

    lax.fori_loop(0, CHUNKS, eliminate, 0)


STREAMS = 22


def compaction(queries, qpos, keys, values, slots):
    vmem = pl.BlockSpec(memory_space=pltpu.VMEM)
    table = pltpu.VMEM((2, RING, SLAB, HALF), BF16)
    wide = pltpu.VMEM((2, RING, SLAB, HALF), F32)
    blocks = pltpu.VMEM((CHUNKS, CHUNKS, LANES, LANES), F32)
    stats = pltpu.VMEM((2, RING, CHUNKS, LANES), F32)
    return pl.pallas_call(
        compaction_kernel,
        out_shape=(
            jax.ShapeDtypeStruct((RING, DH), BF16),
            jax.ShapeDtypeStruct((BLOCK, DH), F32),
        ),
        in_specs=[pl.BlockSpec(memory_space=pltpu.HBM)] * 5,
        out_specs=(vmem,) * 2,
        scratch_shapes=[
            pltpu.SMEM((1, RING), jnp.int32),
            pltpu.VMEM((RING, DH), BF16),
            pltpu.VMEM((BLOCK, DH), BF16),
            pltpu.VMEM((BLOCK, DH), BF16),
            pltpu.VMEM((1, BLOCK), jnp.int32),
            pltpu.VMEM((2, RING, QROWS, DH), F32),
            pltpu.VMEM((2, RING, RING * QROWS, DH), BF16),
            pltpu.VMEM((RING, CHUNKS, LANES), jnp.int32),
            pltpu.VMEM((RING, CHUNKS, LANES), jnp.int32),
            table, table, table, table,
            pltpu.VMEM((DH, BLOCK), BF16),
            wide, wide, stats, wide, stats, table,
            pltpu.VMEM((BLOCK, BLOCK), BF16),
            blocks,
            pltpu.VMEM((CHUNKS, LANES, LANES), F32),
            blocks, blocks,
            pltpu.VMEM((CHUNKS, LANES, LANES), F32),
            pltpu.VMEM((LANES, DH), F32),
            pltpu.VMEM((LANES, LANES), F32),
            pltpu.VMEM((LANES, LANES), F32),
            pltpu.VMEM((BLOCK, LANES), jnp.int32),
            pltpu.SemaphoreType.DMA((5,)),
            pltpu.SemaphoreType.DMA((STREAMS,)),
            pltpu.SemaphoreType.DMA((STREAMS,)),
        ],
        compiler_params=pltpu.CompilerParams(collective_id=0, has_side_effects=True, vmem_limit_bytes=VMEM_LIMIT),
        name="compaction",
    )(qpos, queries, keys, values, slots)


VMEM_LIMIT = 32 * 1024 * 1024


def emit_kernel(own_ref, fitted_ref, own_out, fitted_out):
    own_out[0] = own_ref[...]
    fitted_out[0] = fitted_ref[...]


def emit(own, fitted):
    vmem = pl.BlockSpec(memory_space=pltpu.VMEM)
    return pl.pallas_call(
        emit_kernel,
        out_shape=(
            jax.ShapeDtypeStruct((1, RING, DH), BF16),
            jax.ShapeDtypeStruct((1, BLOCK, DH), F32),
        ),
        in_specs=[vmem] * 2,
        out_specs=(vmem,) * 2,
        compiler_params=pltpu.CompilerParams(vmem_limit_bytes=VMEM_LIMIT),
        name="emit",
    )(own, fitted)


def shards(ref_queries, query_pos, cache_keys, cache_values, slot_index):
    own, fitted = compaction(*(
        pltpu.with_memory_space_constraint(x, pltpu.HBM)
        for x in (ref_queries[0], query_pos, cache_keys[0], cache_values[0], slot_index)
    ))
    return emit(own, fitted)


def solution(mesh):
    in_specs = (
        P("head", "pos", None),
        P("head", "pos"),
        P("head", "pos", None),
        P("head", "pos", None),
        P("head", None),
    )
    out_specs = (P("head", "pos", None), P("head", None, None))
    return jax.shard_map(shards, mesh=mesh, in_specs=in_specs, out_specs=out_specs, check_vma=False)
```
